32 devices in a mesh: fsdp: 16 (over z, x, core), tp: 2 (over y).
Axes of the slice: x: 2, y: 2, z: 4, core: 2. Of those that a mesh axis runs over, the one named last changes fastest.
Arguments:
- tokens: bfloat16 [16384, 768], P(('fsdp', 'tp')), may hold values from -6 to 6
- norm_gain: float32 [768], replicated, may hold values from 0.5 to 1.5
- z_weight: bfloat16 [768, 1536], P('fsdp', 'tp'), may hold values from -0.21875 to 0.21875
- x_weight: bfloat16 [768, 1536], P('fsdp', 'tp'), may hold values from -0.21875 to 0.21875
- bc_weight: bfloat16 [768, 256], P('fsdp'), may hold values from -0.21875 to 0.21875
- dt_weight: bfloat16 [768, 24], P('fsdp', 'tp'), may hold values from -0.21875 to 0.21875
- x_kernel: float32 [4, 1536], P(None, 'tp'), may hold values from -3 to 3
- x_bias: float32 [1536], P('tp'), may hold values from -3 to 3
- bc_kernel: float32 [4, 256], replicated, may hold values from -3 to 3
- bc_bias: float32 [256], replicated, may hold values from -3 to 3
- dt_bias: float32 [24], P('tp'), may hold values from -5 to -1
- decay_log: float32 [24], P('tp'), may hold values from -3 to 1
- skip_gain: float32 [24], P('tp'), may hold values from 0.5 to 1.5
- out_gain: float32 [1536], P('tp'), may hold values from 0.5 to 1.5
- out_weight: bfloat16 [768, 1536], P('fsdp', 'tp'), may hold values from -0.15625 to 0.15625
- cotangent: bfloat16 [16384, 768], P(('fsdp', 'tp')), may hold values from -6 to 6
Outputs:
- output: bfloat16 [16384, 768], P(('fsdp', 'tp'))
- d_tokens: bfloat16 [16384, 768], P(('fsdp', 'tp'))
- d_norm_gain: float32 [768], replicated
- d_z_weight: float32 [768, 1536], P('fsdp', 'tp')
- d_x_weight: float32 [768, 1536], P('fsdp', 'tp')
- d_bc_weight: float32 [768, 256], P('fsdp')
- d_dt_weight: float32 [768, 24], P('fsdp', 'tp')
- d_x_kernel: float32 [4, 1536], P(None, 'tp')
- d_x_bias: float32 [1536], P('tp')
- d_bc_kernel: float32 [4, 256], replicated
- d_bc_bias: float32 [256], replicated
- d_dt_bias: float32 [24], P('tp')
- d_decay_log: float32 [24], P('tp')
- d_skip_gain: float32 [24], P('tp')
- d_out_gain: float32 [1536], P('tp')
- d_out_weight: float32 [768, 1536], P('fsdp', 'tp')
The draws below stay inside these ranges and needn't reach their ends.
All inputs are finite; a program needn't handle non-finite values.
Results may differ from the reference program's by a relative error of at most 0.023.
Values may be sent and summed in bfloat16 or wider, within the bound.
A program may use at most 128 MiB of HBM per device.

```python
import math
import jax
import jax.numpy as jnp
from jax import lax

D = 768
NHEADS = 24
HEADDIM = 64
NSTATE = 128
CONV = 4
SCAN_BLOCK = 256
LEN = 512
INNER = 1536
SEQS = 32
TOKENS = 16384


def levels(own_key, dims, shards, low, top_value):
    loudness, own = 1.0, jax.random.fold_in(own_key, 6)
    for position, blocks in shards:
        draws = jnp.exp(jax.random.uniform(jax.random.fold_in(own, position), (blocks,), jnp.float32, low / len(shards), top_value / len(shards)))
        loudness = loudness * jnp.repeat(draws, dims[position] // blocks).reshape([-1 if axis == position else 1 for axis in range(len(dims))])
    return loudness


def scatter_about(own_key, extent, width, reach, pieces=(), kind=jnp.bfloat16):
    values = width * jax.random.normal(own_key, extent, jnp.float32)
    if pieces:
        values = values * levels(own_key, extent, pieces, -0.22, 0.18)
    return jnp.clip(values, -reach, reach).astype(kind)


def setup_inputs(seed: int = 0) -> dict:
    streams_of = jax.random.split(jax.random.key(seed), 17)
    tokens = scatter_about(streams_of[0], (TOKENS, D), 1.0, 6.0, ((0, 32),))
    norm_gain = jnp.clip(1.0 + 0.1 * jax.random.normal(streams_of[1], (D,), jnp.float32), 0.5, 1.5)
    z_weight = scatter_about(streams_of[2], (D, INNER), D ** -0.5, 0.21875, ((0, 16), (1, 2)))
    x_weight = scatter_about(streams_of[3], (D, INNER), D ** -0.5, 0.21875, ((0, 16), (1, 2)))
    bc_weight = scatter_about(streams_of[4], (D, 2 * NSTATE), D ** -0.5, 0.21875, ((0, 16),))
    dt_weight = scatter_about(streams_of[5], (D, NHEADS), D ** -0.5, 0.21875, ((0, 16), (1, 2)))
    x_kernel = scatter_about(streams_of[6], (CONV, INNER), 0.5, 3.0, ((1, 2),), jnp.float32)
    x_bias = scatter_about(streams_of[7], (INNER,), 0.3, 3.0, ((0, 2),), jnp.float32)
    bc_kernel = scatter_about(streams_of[8], (CONV, 2 * NSTATE), 0.5, 3.0, (), jnp.float32)
    bc_bias = scatter_about(streams_of[9], (2 * NSTATE,), 0.3, 3.0, (), jnp.float32)
    dt_bias = jnp.clip(-5.0 + 4.0 * jax.random.uniform(streams_of[10], (NHEADS,), jnp.float32) ** levels(streams_of[10], (NHEADS,), ((0, 2),), -0.2, 0.2), -5.0, -1.0)
    decay_log = jnp.clip(-3.0 + 4.0 * jax.random.uniform(streams_of[11], (NHEADS,), jnp.float32) ** levels(streams_of[11], (NHEADS,), ((0, 2),), -0.2, 0.2), -3.0, 1.0)
    skip_gain = jnp.clip(0.5 + 1.0 * jax.random.uniform(streams_of[12], (NHEADS,), jnp.float32) ** levels(streams_of[12], (NHEADS,), ((0, 2),), -0.2, 0.2), 0.5, 1.5)
    out_gain = jnp.clip(1.0 + 0.1 * jax.random.normal(streams_of[13], (INNER,), jnp.float32), 0.5, 1.5)
    out_weight = scatter_about(streams_of[14], (D, INNER), INNER ** -0.5, 0.15625, ((0, 16), (1, 2)))
    cotangent = scatter_about(streams_of[15], (TOKENS, D), 1.0, 6.0, ((0, 32),))
    return {"tokens": tokens, "norm_gain": norm_gain, "z_weight": z_weight, "x_weight": x_weight, "bc_weight": bc_weight, "dt_weight": dt_weight, "x_kernel": x_kernel, "x_bias": x_bias, "bc_kernel": bc_kernel, "bc_bias": bc_bias, "dt_bias": dt_bias, "decay_log": decay_log, "skip_gain": skip_gain, "out_gain": out_gain, "out_weight": out_weight, "cotangent": cotangent}


epsilon = 1e-05
highest = lax.Precision.HIGHEST

@jax.custom_vjp
def low(v):
    return lax.optimization_barrier(v.astype(jnp.bfloat16)).astype(jnp.float32)

@jax.custom_vjp
def low_back(v):
    return v

def low_keep(v):
    return (low(v), None)

def low_pass(kept, grad):
    return (grad,)

def back_keep(v):
    return (v, None)

def back_low(kept, grad):
    return (low(grad),)
low.defvjp(low_keep, low_pass)
low_back.defvjp(back_keep, back_low)

def causal_conv(series, kernel, offset_bias):
    length = series.shape[1]
    padded = jnp.pad(series, ((0, 0), (CONV - 1, 0), (0, 0)))
    summed = jnp.zeros(series.shape, jnp.float32) + offset_bias
    for shift_pos in range(CONV):
        summed = summed + kernel[shift_pos] * padded[:, shift_pos:shift_pos + length]
    return jax.nn.silu(summed)

def ssd_scan(values_in, delta, rates, b_proj, c_proj):
    seq_count, length, head_count, head_size = values_in.shape
    block_total = length // SCAN_BLOCK
    values = values_in.reshape(seq_count, block_total, SCAN_BLOCK, head_count, head_size)
    steps_dt = delta.reshape(seq_count, block_total, SCAN_BLOCK, head_count)
    b_blocks = b_proj.reshape(seq_count, block_total, SCAN_BLOCK, -1)
    c_blocks = c_proj.reshape(seq_count, block_total, SCAN_BLOCK, -1)
    cumulative = jnp.cumsum(steps_dt * rates, axis=2)
    by_head = jnp.transpose(cumulative, (0, 1, 3, 2))
    dt_head = jnp.transpose(steps_dt, (0, 1, 3, 2))
    places = jnp.arange(SCAN_BLOCK)
    causal = places[:, None] >= places[None, :]
    gaps = by_head[..., :, None] - by_head[..., None, :]
    weights = jnp.exp(jnp.where(causal, gaps, -1e+30))
    scores = jnp.einsum('skqn,skrn->skqr', c_blocks, b_blocks, precision=highest)
    mixing = scores[:, :, None] * weights * dt_head[..., None, :]
    within = jnp.einsum('skhqr,skrhp->skqhp', mixing, values, precision=highest)
    to_end = jnp.exp(cumulative[:, :, -1:, :] - cumulative) * steps_dt
    block_states = jnp.einsum('skrh,skrhp,skrn->skhpn', to_end, values, b_blocks, precision=highest)
    fading = jnp.exp(cumulative[:, :, -1, :])
    running = jnp.zeros(block_states.shape[:1] + block_states.shape[2:], jnp.float32)
    entering = []
    for block_pos in range(block_total):
        entering.append(running)
        running = running * fading[:, block_pos, :, None, None] + block_states[:, block_pos]
    entering = jnp.stack(entering, 1)
    across = jnp.einsum('skqn,skhpn->skqhp', c_blocks, entering, precision=highest) * jnp.exp(cumulative)[..., None]
    return (within + across).reshape(seq_count, length, head_count, head_size)

def high_dot(left, right):
    return jnp.dot(left, right, precision=highest, preferred_element_type=jnp.float32)

def layer_forward(row_block, norm_gain, z_weight, x_weight, bc_weight, dt_weight, x_kernel, x_bias, bc_kernel, bc_bias, dt_bias, decay_log, skip_gain, out_gain, out_weight):
    seq_count = row_block.shape[0] // LEN
    inverse = lax.rsqrt(lax.optimization_barrier(jnp.mean(row_block * row_block, -1, keepdims=True)) + epsilon)
    normed = low(row_block * inverse * norm_gain)
    gate_raw = low_back(low(high_dot(normed, z_weight)))
    x_raw = low_back(low(high_dot(normed, x_weight)))
    bc_raw = low_back(low(high_dot(normed, bc_weight)))
    dt_raw = low_back(low(high_dot(normed, dt_weight)))
    x_conv = low(causal_conv(x_raw.reshape(seq_count, LEN, INNER), x_kernel, x_bias))
    bc_conv = low(causal_conv(bc_raw.reshape(seq_count, LEN, 2 * NSTATE), bc_kernel, bc_bias))
    heads_in = x_conv.reshape(seq_count, LEN, NHEADS, HEADDIM)
    delta = jax.nn.softplus(dt_raw.reshape(seq_count, LEN, NHEADS) + dt_bias)
    result = ssd_scan(heads_in, delta, -jnp.exp(decay_log), bc_conv[..., :NSTATE], bc_conv[..., NSTATE:])
    result = result + skip_gain[:, None] * heads_in
    gated = result.reshape(-1, INNER) * jax.nn.silu(gate_raw)
    scale = lax.rsqrt(lax.optimization_barrier(jnp.mean(gated * gated, -1, keepdims=True)) + epsilon)
    mixed = low(gated * scale * out_gain)
    return row_block + high_dot(mixed, out_weight.T)

def reference(tokens, norm_gain, z_weight, x_weight, bc_weight, dt_weight, x_kernel, x_bias, bc_kernel, bc_bias, dt_bias, decay_log, skip_gain, out_gain, out_weight, cotangent):
    floats = tuple((item.astype(jnp.float32) for item in (norm_gain, z_weight, x_weight, bc_weight, dt_weight, x_kernel, x_bias, bc_kernel, bc_bias, dt_bias, decay_log, skip_gain, out_gain, out_weight)))
    per_block = math.gcd(SEQS, max(1, 4096 // LEN))
    block_count = SEQS // per_block
    inputs = tokens.astype(jnp.float32).reshape(block_count, per_block * LEN, D)
    cots = cotangent.astype(jnp.float32).reshape(block_count, per_block * LEN, D)

    def scan_step(totals, pair):
        piece, cot_piece = pair
        result, pull = jax.vjp(layer_forward, piece, *floats)
        grads = pull(cot_piece)
        totals = tuple((acc + grad for acc, grad in zip(totals, grads[1:])))
        return (totals, (result.astype(jnp.bfloat16), grads[0].astype(jnp.bfloat16)))
    start = tuple((jnp.zeros_like(item) for item in floats))
    sums, (outputs, d_inputs) = lax.scan(scan_step, start, (inputs, cots))
    return (outputs.reshape(TOKENS, D), d_inputs.reshape(TOKENS, D)) + tuple(sums)
```

```python
import functools

import jax
import jax.numpy as jnp
from jax import lax
from jax.experimental import pallas as pl
from jax.experimental.pallas import tpu as pltpu
from jax.sharding import PartitionSpec as P

HEADDIM = 64
NSTATE = 128
CONV = 4
SCAN_BLOCK = 256
LEN = 512
INNER = 1536


epsilon = 1e-05
highest = lax.Precision.HIGHEST
DT_PAD = 128


def causal_conv(series, kernel, offset_bias):
    length = series.shape[1]
    padded = jnp.pad(series, ((0, 0), (CONV - 1, 0), (0, 0)))
    summed = jnp.zeros(series.shape, jnp.float32) + offset_bias
    for shift_pos in range(CONV):
        summed = summed + kernel[shift_pos] * padded[:, shift_pos : shift_pos + length]
    return jax.nn.silu(summed)


def ssd_scan(values_in, delta, rates, b_proj, c_proj):
    seq_count, length, head_count, head_size = values_in.shape
    block_total = length // SCAN_BLOCK
    values = values_in.reshape(seq_count, block_total, SCAN_BLOCK, head_count, head_size)
    steps_dt = delta.reshape(seq_count, block_total, SCAN_BLOCK, head_count)
    b_blocks = b_proj.reshape(seq_count, block_total, SCAN_BLOCK, -1)
    c_blocks = c_proj.reshape(seq_count, block_total, SCAN_BLOCK, -1)
    cumulative = jnp.cumsum(steps_dt * rates, axis=2)
    by_head = jnp.transpose(cumulative, (0, 1, 3, 2))
    dt_head = jnp.transpose(steps_dt, (0, 1, 3, 2))
    places = jnp.arange(SCAN_BLOCK)
    causal = places[:, None] >= places[None, :]
    gaps = by_head[..., :, None] - by_head[..., None, :]
    weights = jnp.exp(jnp.where(causal, gaps, -1e30))
    scores = jnp.einsum("skqn,skrn->skqr", c_blocks, b_blocks, precision=highest)
    mixing = scores[:, :, None] * weights * dt_head[..., None, :]
    within = jnp.einsum("skhqr,skrhp->skqhp", mixing, values, precision=highest)
    to_end = jnp.exp(cumulative[:, :, -1:, :] - cumulative) * steps_dt
    block_states = jnp.einsum("skrh,skrhp,skrn->skhpn", to_end, values, b_blocks, precision=highest)
    fading = jnp.exp(cumulative[:, :, -1, :])
    running = jnp.zeros(block_states.shape[:1] + block_states.shape[2:], jnp.float32)
    entering = []
    for block_pos in range(block_total):
        entering.append(running)
        running = running * fading[:, block_pos, :, None, None] + block_states[:, block_pos]
    entering = jnp.stack(entering, 1)
    across = (
        jnp.einsum("skqn,skhpn->skqhp", c_blocks, entering, precision=highest)
        * jnp.exp(cumulative)[..., None]
    )
    return (within + across).reshape(seq_count, length, head_count, head_size)


def prenorm(row_block, norm_gain):
    inverse = lax.rsqrt(jnp.mean(row_block * row_block, -1, keepdims=True) + epsilon)
    return row_block * inverse * norm_gain


def conv_piece(x_raw, bc_raw, x_kernel, x_bias, bc_kernel, bc_bias):
    seq_count = x_raw.shape[0] // LEN
    x_conv = causal_conv(x_raw.reshape(seq_count, LEN, -1), x_kernel, x_bias)
    bc_conv = causal_conv(bc_raw.reshape(seq_count, LEN, -1), bc_kernel, bc_bias)
    return (x_conv.reshape(x_raw.shape), bc_conv.reshape(bc_raw.shape))


def mixer_piece(x_conv, bc_conv, dt_raw, gate_raw, dt_bias, decay_log, skip_gain):
    row_count = x_conv.shape[0]
    seq_count = row_count // LEN
    head_count = dt_raw.shape[1]
    heads_in = x_conv.reshape(seq_count, LEN, head_count, HEADDIM)
    delta = jax.nn.softplus(dt_raw.reshape(seq_count, LEN, head_count) + dt_bias)
    bc_seq = bc_conv.reshape(seq_count, LEN, 2 * NSTATE)
    result = ssd_scan(
        heads_in, delta, -jnp.exp(decay_log), bc_seq[..., :NSTATE], bc_seq[..., NSTATE:]
    )
    result = result + skip_gain[:, None] * heads_in
    return result.reshape(row_count, -1) * jax.nn.silu(gate_raw)


def rounded(value):
    return lax.optimization_barrier(value.astype(jnp.bfloat16)).astype(jnp.float32)


def contract_rows(left, right):
    return lax.dot_general(
        left, right, (((0,), (0,)), ((), ())), preferred_element_type=jnp.float32
    )


def contract_cols(left, right):
    return lax.dot_general(
        left, right, (((1,), (1,)), ((), ())), preferred_element_type=jnp.float32
    )


def project(rows_in, matrix):
    return jnp.dot(rows_in, matrix, preferred_element_type=jnp.float32).astype(jnp.bfloat16)


def local(
    tokens,
    norm_gain,
    z_weight,
    x_weight,
    bc_weight,
    dt_weight,
    x_kernel,
    x_bias,
    bc_kernel,
    bc_bias,
    dt_bias,
    decay_log,
    skip_gain,
    out_gain,
    out_weight,
    cotangent,
):
    residual = tokens.astype(jnp.float32)
    normed, norm_pull = jax.vjp(prenorm, residual, norm_gain)
    normed_low = normed.astype(jnp.bfloat16)
    full_rows = lax.all_gather(normed_low, "tp", axis=0, tiled=True)
    gathered = (
        lax.all_gather(z_weight, "fsdp", axis=0, tiled=True),
        lax.all_gather(x_weight, "fsdp", axis=0, tiled=True),
        lax.all_gather(bc_weight, "fsdp", axis=0, tiled=True),
        lax.all_gather(dt_weight, "fsdp", axis=0, tiled=True),
        lax.all_gather(out_weight, "fsdp", axis=0, tiled=True),
    )
    z_full, x_full, bc_full, dt_full, out_full = gathered
    gate_low = project(full_rows, z_full)
    xraw_low = project(full_rows, x_full)
    bcraw_low = project(full_rows, bc_full)
    dtraw_low = project(full_rows, dt_full)
    (x_conv, bc_conv), conv_pull = jax.vjp(
        conv_piece,
        xraw_low.astype(jnp.float32),
        bcraw_low.astype(jnp.float32),
        x_kernel,
        x_bias,
        bc_kernel,
        bc_bias,
    )
    x_round = rounded(x_conv)
    bc_round = rounded(bc_conv)
    gated, mixer_pull = jax.vjp(
        mixer_piece,
        x_round,
        bc_round,
        dtraw_low.astype(jnp.float32),
        gate_low.astype(jnp.float32),
        dt_bias,
        decay_log,
        skip_gain,
    )
    square_part = jnp.sum(gated * gated, -1)
    square_sum = lax.psum(square_part, "tp")
    scale = lax.rsqrt(square_sum / INNER + epsilon)[:, None]
    mixed_low = (gated * scale * out_gain).astype(jnp.bfloat16)
    branch = contract_cols(mixed_low, out_full)
    branch_rows = lax.psum_scatter(branch, "tp", scatter_dimension=0, tiled=True)
    output = (residual + branch_rows).astype(jnp.bfloat16)
    cot_rows = lax.all_gather(cotangent, "tp", axis=0, tiled=True)
    d_out_weight = contract_rows(cot_rows, mixed_low)
    d_mixed = jnp.dot(cot_rows, out_full, preferred_element_type=jnp.float32)
    d_out_gain = jnp.sum(d_mixed * gated * scale, 0)
    scaled_grad = d_mixed * out_gain
    cross_part = jnp.sum(scaled_grad * gated, -1)
    cross_sum = lax.psum(cross_part, "tp")
    d_gated = scale * scaled_grad - gated * scale**3 * (cross_sum / INNER)[:, None]
    d_x_round, d_bc_part, d_dt_raw, d_gate_raw, d_dt_bias, d_decay_log, d_skip_gain = mixer_pull(
        d_gated
    )
    d_bc_round = lax.psum(d_bc_part, "tp")
    d_x_raw, d_bc_raw, d_x_kernel, d_x_bias, d_bc_kernel, d_bc_bias = conv_pull(
        (d_x_round, d_bc_round)
    )
    gate_grad = d_gate_raw.astype(jnp.bfloat16)
    xraw_grad = d_x_raw.astype(jnp.bfloat16)
    bcraw_grad = d_bc_raw.astype(jnp.bfloat16)
    dtraw_grad = d_dt_raw.astype(jnp.bfloat16)
    d_z_weight = contract_rows(full_rows, gate_grad)
    d_x_weight = contract_rows(full_rows, xraw_grad)
    d_bc_weight = contract_rows(full_rows, bcraw_grad)
    d_dt_weight = contract_rows(full_rows, dtraw_grad)
    input_part = contract_cols(gate_grad, z_full) + contract_cols(xraw_grad, x_full)
    input_part = input_part + contract_cols(dtraw_grad, dt_full)
    input_rows = lax.psum_scatter(input_part, "tp", scatter_dimension=0, tiled=True)
    own_count = tokens.shape[0]
    own_bc = lax.dynamic_slice_in_dim(bcraw_grad, lax.axis_index("tp") * own_count, own_count, 0)
    d_normed = input_rows + contract_cols(own_bc, bc_full)
    d_residual, d_norm_part = norm_pull(d_normed)
    d_tokens = (cotangent.astype(jnp.float32) + d_residual).astype(jnp.bfloat16)
    d_z_weight, d_x_weight, d_bc_weight, d_dt_weight, d_out_weight = (
        lax.psum_scatter(d_z_weight, "fsdp", scatter_dimension=0, tiled=True),
        lax.psum_scatter(d_x_weight, "fsdp", scatter_dimension=0, tiled=True),
        lax.psum_scatter(d_bc_weight, "fsdp", scatter_dimension=0, tiled=True),
        lax.psum_scatter(d_dt_weight, "fsdp", scatter_dimension=0, tiled=True),
        lax.psum_scatter(d_out_weight, "fsdp", scatter_dimension=0, tiled=True),
    )
    (
        d_x_kernel,
        d_x_bias,
        d_bc_kernel,
        d_bc_bias,
        d_dt_bias,
        d_decay_log,
        d_skip_gain,
        d_out_gain,
    ) = lax.psum(
        (
            d_x_kernel,
            d_x_bias,
            d_bc_kernel,
            d_bc_bias,
            d_dt_bias,
            d_decay_log,
            d_skip_gain,
            d_out_gain,
        ),
        "fsdp",
    )
    d_norm_gain = lax.psum(d_norm_part, ("fsdp", "tp"))
    return (
        output,
        d_tokens,
        d_norm_gain,
        d_z_weight,
        d_x_weight,
        d_bc_weight,
        d_dt_weight,
        d_x_kernel,
        d_x_bias,
        d_bc_kernel,
        d_bc_bias,
        d_dt_bias,
        d_decay_log,
        d_skip_gain,
        d_out_gain,
        d_out_weight,
    )


def bits_of(count):
    return [1 << k for k in range(count.bit_length() - 1)]


def orders_of(fsdp_count, tp_count):
    own = bits_of(fsdp_count)
    other = [bit * fsdp_count for bit in bits_of(tp_count)]
    return (own[:2] + other + own[2:], own[:1] + other + own[1:])


def flipped(mask, fsdp_count, f_pos, t_pos):
    low, high = mask % fsdp_count, mask // fsdp_count
    for bit in bits_of(fsdp_count):
        if low & bit:
            f_pos = f_pos + bit - 2 * bit * ((lax.axis_index("fsdp") // bit) % 2)
    bit = 1
    while bit <= high:
        if high & bit:
            t_pos = t_pos + bit - 2 * bit * ((lax.axis_index("tp") // bit) % 2)
        bit *= 2
    return f_pos, t_pos


def greet(all_bits, place):
    barrier = pltpu.get_barrier_semaphore()
    for bit in all_bits:
        pl.semaphore_signal(
            barrier, inc=1, device_id=place(bit), device_id_type=pl.DeviceIdType.MESH
        )
    pl.semaphore_wait(barrier, len(all_bits))


def gather_kernel(
    fsdp_count, tp_count, shard, small, full, small_full, send_sem, recv_sem, near_sem,
    small_send, small_recv,
):
    f_own, t_own = lax.axis_index("fsdp"), lax.axis_index("tp")
    place = lambda mask: flipped(mask, fsdp_count, f_own, t_own)

    def slot(mask):
        f_pos, t_pos = place(mask)
        return t_pos * fsdp_count + f_pos

    total = fsdp_count * tp_count
    forward = orders_of(fsdp_count, tp_count)
    greet(forward[0], place)
    half = shard.shape[1] // 2
    pending = []

    def send(lane, mask, bit):
        cols = pl.ds(lane * half, half)
        source = shard.at[:, cols] if mask == 0 else full.at[slot(mask), :, cols]
        copy = pltpu.make_async_remote_copy(
            src_ref=source,
            dst_ref=full.at[slot(mask), :, cols],
            send_sem=send_sem.at[lane, mask + bit],
            recv_sem=recv_sem.at[lane, mask + bit],
            device_id=place(bit),
            device_id_type=pl.DeviceIdType.MESH,
        )
        copy.start()
        pending.append(copy)
        return copy

    arriving = {}
    orders = [list(reversed(order)) for order in forward]
    for lane in range(2):
        for bit in orders[lane]:
            arriving[lane, bit] = send(lane, 0, bit)
    near = pltpu.make_async_copy(shard, full.at[slot(0)], near_sem.at[0])
    near.start()
    near_small = pltpu.make_async_copy(small, small_full.at[t_own], near_sem.at[1])
    near_small.start()
    small_copies = []
    for t_mask in range(1, tp_count):
        copy = pltpu.make_async_remote_copy(
            src_ref=small,
            dst_ref=small_full.at[t_own],
            send_sem=small_send.at[t_mask],
            recv_sem=small_recv.at[t_mask],
            device_id=place(t_mask * fsdp_count),
            device_id_type=pl.DeviceIdType.MESH,
        )
        copy.start()
        small_copies.append(copy)
    held = [[0], [0]]
    for stage in range(len(forward[0])):
        for lane in range(2):
            bit = orders[lane][stage]
            later = orders[lane][stage + 1 :]
            for mask in list(held[lane]):
                arriving[lane, mask + bit].wait_recv()
                held[lane].append(mask + bit)
                for next_bit in later:
                    arriving[lane, mask + bit + next_bit] = send(lane, mask + bit, next_bit)
    for copy in small_copies:
        copy.wait()
    for copy in pending:
        copy.wait_send()
    near.wait()
    near_small.wait()


def gather_all(shard, small, fsdp_count, tp_count):
    total = fsdp_count * tp_count
    return pl.pallas_call(
        functools.partial(gather_kernel, fsdp_count, tp_count),
        out_shape=(
            jax.ShapeDtypeStruct((total,) + shard.shape, shard.dtype),
            jax.ShapeDtypeStruct((tp_count,) + small.shape, small.dtype),
        ),
        in_specs=[pl.BlockSpec(memory_space=pltpu.VMEM)] * 2,
        out_specs=(pl.BlockSpec(memory_space=pltpu.VMEM),) * 2,
        scratch_shapes=[
            pltpu.SemaphoreType.DMA((2, total)),
            pltpu.SemaphoreType.DMA((2, total)),
            pltpu.SemaphoreType.DMA((2,)),
            pltpu.SemaphoreType.DMA((tp_count,)),
            pltpu.SemaphoreType.DMA((tp_count,)),
        ],
        compiler_params=pltpu.CompilerParams(
            collective_id=0, has_side_effects=True, vmem_limit_bytes=40 << 20
        ),
        name="gather_weights",
    )(shard, small)


def reduce_kernel(
    fsdp_count, tp_count, lanes, first, second, small, first_out, second_out, small_out,
    first_got, second_got, first_sum, second_sum, small_sum, small_got,
    send_sem, recv_sem, small_send, small_recv,
):
    f_own, t_own = lax.axis_index("fsdp"), lax.axis_index("tp")
    place = lambda mask: flipped(mask, fsdp_count, f_own, t_own)

    def slot(mask):
        f_pos, t_pos = place(mask)
        return t_pos * fsdp_count + f_pos

    total = fsdp_count * tp_count
    both = orders_of(fsdp_count, tp_count)
    greet(both[0], place)
    parts = ((first, first_got, first_sum, first_out), (second, second_got, second_sum, second_out))
    stages = len(both[0])
    pending = []
    arriving = {}
    small_copies = []
    for stage in range(stages + 1):
        if stage < stages:
            bit = both[0][stage]
            source = small if stage == 0 else small_sum.at[stage - 1]
            small_copy = pltpu.make_async_remote_copy(
                src_ref=source,
                dst_ref=small_got.at[stage],
                send_sem=small_send.at[stage],
                recv_sem=small_recv.at[stage],
                device_id=place(bit),
                device_id_type=pl.DeviceIdType.MESH,
            )
            small_copy.start()
            pending.append(small_copy)
        for lane, (which, start, size, order_pos) in enumerate(lanes):
            given, got, held, out = parts[which]
            order = both[order_pos]
            cols = pl.ds(start, size)
            kept = [m for m in range(total) if not any(m & b for b in order[:stage])]
            if stage > 0:
                previous = order[stage - 1]
                now = order[stage] if stage < stages else 0
                kept = sorted(kept, key=lambda m: not (m & now))
            for mask in kept:
                if stage > 0:
                    arriving[lane, mask + previous].wait_recv()
                    before = given[slot(mask), :, cols] if stage == 1 else held[mask // 2, :, cols]
                    add = got[mask + previous, :, cols]
                    if stage == stages:
                        out[:, cols] = before.astype(jnp.float32) + add.astype(jnp.float32)
                    else:
                        held[mask // 2, :, cols] = before + add
                if stage < stages and mask & order[stage]:
                    source = (
                        given.at[slot(mask), :, cols]
                        if stage == 0
                        else held.at[mask // 2, :, cols]
                    )
                    copy = pltpu.make_async_remote_copy(
                        src_ref=source,
                        dst_ref=got.at[mask, :, cols],
                        send_sem=send_sem.at[lane, mask],
                        recv_sem=recv_sem.at[lane, mask],
                        device_id=place(order[stage]),
                        device_id_type=pl.DeviceIdType.MESH,
                    )
                    copy.start()
                    pending.append(copy)
                    arriving[lane, mask] = copy
        if stage < stages:
            small_copy.wait_recv()
            before = small[...] if stage == 0 else small_sum[stage - 1]
            if stage == stages - 1:
                small_out[...] = before + small_got[stage]
            else:
                small_sum[stage] = before + small_got[stage]
    for copy in pending:
        copy.wait_send()


def reduce_all(first, second, small, fsdp_count, tp_count):
    total, rows, wide = first.shape
    narrow = second.shape[2]
    cut = (wide * 3 // 5) // 128 * 128
    lanes = ((1, 0, narrow, 0), (0, 0, cut, 1), (0, cut, wide - cut, 0))
    stages = total.bit_length() - 1
    low = jnp.bfloat16
    return pl.pallas_call(
        functools.partial(reduce_kernel, fsdp_count, tp_count, lanes),
        out_shape=(
            jax.ShapeDtypeStruct((rows, wide), jnp.float32),
            jax.ShapeDtypeStruct((rows, narrow), jnp.float32),
            jax.ShapeDtypeStruct(small.shape, jnp.float32),
        ),
        in_specs=[pl.BlockSpec(memory_space=pltpu.VMEM)] * 3,
        out_specs=(pl.BlockSpec(memory_space=pltpu.VMEM),) * 3,
        scratch_shapes=[
            pltpu.VMEM((total, rows, wide), low),
            pltpu.VMEM((total, rows, narrow), low),
            pltpu.VMEM((total // 2, rows, wide), low),
            pltpu.VMEM((total // 2, rows, narrow), low),
            pltpu.VMEM((stages,) + small.shape, jnp.float32),
            pltpu.VMEM((stages,) + small.shape, jnp.float32),
            pltpu.SemaphoreType.DMA((len(lanes), total)),
            pltpu.SemaphoreType.DMA((len(lanes), total)),
            pltpu.SemaphoreType.DMA((stages,)),
            pltpu.SemaphoreType.DMA((stages,)),
        ],
        compiler_params=pltpu.CompilerParams(
            collective_id=1, has_side_effects=True, vmem_limit_bytes=48 << 20
        ),
        name="reduce_gradients",
    )(first, second, small)


def pad_cols(value, width):
    return jnp.pad(value, ((0, 0), (0, width - value.shape[1])))


def by_sequence(
    fsdp_count,
    tp_count,
    tokens,
    norm_gain,
    z_weight,
    x_weight,
    bc_weight,
    dt_weight,
    x_kernel,
    x_bias,
    bc_kernel,
    bc_bias,
    dt_bias,
    decay_log,
    skip_gain,
    out_gain,
    out_weight,
    cotangent,
):
    rows, width = z_weight.shape
    heads = dt_weight.shape[1]
    depth = tokens.shape[1]
    count = tokens.shape[0]
    bc_share = 2 * NSTATE // tp_count
    bc_own = lax.dynamic_slice_in_dim(bc_weight, lax.axis_index("tp") * bc_share, bc_share, 1)
    shard = jnp.concatenate(
        [z_weight, x_weight, pad_cols(dt_weight, DT_PAD), bc_own, out_weight], 1
    )
    small = jnp.concatenate(
        [
            x_kernel,
            x_bias[None],
            out_gain[None],
            pad_cols(jnp.concatenate([dt_bias, decay_log, skip_gain])[None], width),
            jnp.zeros((1, width), jnp.float32),
        ],
        0,
    )
    full, small_full = gather_all(shard, small, fsdp_count, tp_count)
    full = full.reshape(tp_count, depth, shard.shape[1])
    out_start = 2 * width + DT_PAD + bc_share
    proj_w, out_w = full[:, :, :out_start], full[:, :, out_start:]
    join = lambda value: jnp.moveaxis(value, 0, -2).reshape(value.shape[1:-1] + (-1,))
    x_kernel_all = join(small_full[:, :CONV])
    x_bias_all = small_full[:, CONV].reshape(-1)
    out_gain_all = small_full[:, CONV + 1]
    tiny = small_full[:, CONV + 2, : 3 * heads].reshape(tp_count, 3, heads)
    dt_bias_all, decay_all, skip_all = (tiny[:, k].reshape(-1) for k in range(3))

    residual = tokens.astype(jnp.float32)
    normed, norm_pull = jax.vjp(prenorm, residual, norm_gain)
    normed_low = normed.astype(jnp.bfloat16)
    raw = jnp.einsum(
        "rk,tkc->trc", normed_low, proj_w, preferred_element_type=jnp.float32
    ).astype(jnp.bfloat16)
    gate_low = join(raw[:, :, :width])
    xraw_low = join(raw[:, :, width : 2 * width])
    dtraw_low = join(raw[:, :, 2 * width : 2 * width + heads])
    bcraw_low = join(raw[:, :, 2 * width + DT_PAD :])
    gated, scan_pull, conv_pull = mixer(
        xraw_low, bcraw_low, dtraw_low, gate_low, x_kernel_all, x_bias_all, bc_kernel, bc_bias,
        dt_bias_all, decay_all, skip_all,
    )
    scale = lax.rsqrt(jnp.sum(gated * gated, -1) / INNER + epsilon)[:, None]
    gain = out_gain_all.reshape(-1)
    mixed_low = (gated * scale * gain).astype(jnp.bfloat16)
    split = lambda value: jnp.moveaxis(value.reshape(value.shape[0], tp_count, -1), 1, 0)
    mixed_split = split(mixed_low)
    branch = jnp.einsum("trc,tkc->rk", mixed_split, out_w, preferred_element_type=jnp.float32)
    output = (residual + branch).astype(jnp.bfloat16)
    d_out_weight = jnp.einsum(
        "rk,trc->tkc", cotangent, mixed_split, preferred_element_type=jnp.float32
    ).astype(jnp.bfloat16)
    d_mixed = jnp.einsum("rk,tkc->trc", cotangent, out_w, preferred_element_type=jnp.float32)
    d_mixed = join(d_mixed)
    d_out_gain = jnp.sum(d_mixed * gated * scale, 0)
    scaled_grad = d_mixed * gain
    cross_sum = jnp.sum(scaled_grad * gated, -1)
    d_gated = scale * scaled_grad - gated * scale**3 * (cross_sum / INNER)[:, None]
    d_x_round, d_bc_round, d_dt_raw, d_gate_raw, d_dt_bias, d_decay_log, d_skip_gain = scan_pull(
        d_gated
    )
    d_x_raw, d_bc_raw, d_x_kernel, d_x_bias, d_bc_kernel, d_bc_bias = conv_pull(
        (d_x_round, d_bc_round)
    )
    low = jnp.bfloat16
    bc_grad = d_bc_raw.astype(low)
    dt_grad = split(d_dt_raw.astype(low))
    dt_grad = jnp.pad(dt_grad, ((0, 0), (0, 0), (0, DT_PAD - heads)))
    lead = jnp.concatenate([split(d_gate_raw.astype(low)), split(d_x_raw.astype(low)), dt_grad], 2)
    proj_grad = jnp.concatenate([lead, split(bc_grad)], 2)
    d_normed = jnp.einsum("trc,tkc->rk", proj_grad, proj_w, preferred_element_type=jnp.float32)
    bc_all = jnp.broadcast_to(bc_grad[None], (tp_count,) + bc_grad.shape)
    d_proj = jnp.einsum(
        "rk,trc->tkc",
        normed_low,
        jnp.concatenate([lead, bc_all], 2),
        preferred_element_type=jnp.float32,
    ).astype(low)
    d_residual, d_norm_gain = norm_pull(d_normed)
    d_tokens = (cotangent.astype(jnp.float32) + d_residual).astype(jnp.bfloat16)
    tiny_grad = jnp.stack([d_dt_bias, d_decay_log, d_skip_gain]).reshape(3, tp_count, heads)
    tiny_grad = jnp.moveaxis(tiny_grad, 1, 0).reshape(tp_count, 3 * heads)
    flat = jnp.concatenate(
        [
            d_norm_gain,
            d_bc_kernel.reshape(-1),
            d_bc_bias,
            d_out_gain,
            d_x_bias,
            d_x_kernel.reshape(-1),
            tiny_grad.reshape(-1),
        ]
    )
    lines = -(-flat.size // width)
    lines = -(-lines // 8) * 8
    small_grad = jnp.pad(flat, (0, lines * width - flat.size)).reshape(lines, width)
    wide, narrow, sums = reduce_all(
        d_proj.reshape(fsdp_count * tp_count, rows, -1),
        d_out_weight.reshape(fsdp_count * tp_count, rows, -1),
        small_grad,
        fsdp_count,
        tp_count,
    )
    sums = sums.reshape(-1)
    t_own = lax.axis_index("tp")
    position = 0

    def take(*shape):
        nonlocal position
        size = 1
        for extent in shape:
            size *= extent
        piece = sums[position : position + size].reshape(shape)
        position += size
        return piece

    own = lambda value: lax.dynamic_index_in_dim(value, t_own, value.ndim - 2, keepdims=False)
    d_norm_gain = take(depth)
    d_bc_kernel = take(CONV, 2 * NSTATE)
    d_bc_bias = take(2 * NSTATE)
    d_out_gain = own(take(tp_count, width))
    d_x_bias = own(take(tp_count, width))
    d_x_kernel = own(take(CONV, tp_count, width))
    d_tiny = own(take(tp_count, 3 * heads)).reshape(3, heads)
    return (
        output,
        d_tokens,
        d_norm_gain,
        wide[:, :width],
        wide[:, width : 2 * width],
        wide[:, 2 * width + DT_PAD :],
        wide[:, 2 * width : 2 * width + heads],
        d_x_kernel,
        d_x_bias,
        d_bc_kernel,
        d_bc_bias,
        d_tiny[0],
        d_tiny[1],
        d_tiny[2],
        d_out_gain,
        narrow,
    )


def mixer(
    xraw_low, bcraw_low, dtraw_low, gate_low, x_kernel, x_bias, bc_kernel, bc_bias, dt_bias,
    decay_log, skip_gain,
):
    (x_conv, bc_conv), conv_pull = jax.vjp(
        conv_piece,
        xraw_low.astype(jnp.float32),
        bcraw_low.astype(jnp.float32),
        x_kernel,
        x_bias,
        bc_kernel,
        bc_bias,
    )
    gated, scan_pull = jax.vjp(
        mixer_piece,
        rounded(x_conv),
        rounded(bc_conv),
        dtraw_low.astype(jnp.float32),
        gate_low.astype(jnp.float32),
        dt_bias,
        decay_log,
        skip_gain,
    )
    return gated, scan_pull, conv_pull


def solution(mesh):
    placed = (
        P(("fsdp", "tp"), None),
        P(),
        P("fsdp", "tp"),
        P("fsdp", "tp"),
        P("fsdp", None),
        P("fsdp", "tp"),
        P(None, "tp"),
        P("tp"),
        P(),
        P(),
        P("tp"),
        P("tp"),
        P("tp"),
        P("tp"),
        P("fsdp", "tp"),
        P(("fsdp", "tp"), None),
    )
    fsdp_count, tp_count = mesh.shape["fsdp"], mesh.shape["tp"]
    total = fsdp_count * tp_count

    def program(*arrays):
        rows, width = arrays[2].shape
        whole = arrays[0].shape[0] % LEN == 0 and 2 * NSTATE % (128 * tp_count) == 0
        tiled = rows % 16 == 0 and width % 128 == 0 and arrays[0].shape[1] == width
        if whole and tiled and total & (total - 1) == 0 and fsdp_count >= 4:
            return by_sequence(fsdp_count, tp_count, *arrays)
        return local(*arrays)

    return jax.shard_map(
        program,
        mesh=mesh,
        in_specs=placed,
        out_specs=(
            P(("fsdp", "tp"), None),
            P(("fsdp", "tp"), None),
            P(),
            P("fsdp", "tp"),
            P("fsdp", "tp"),
            P("fsdp", None),
            P("fsdp", "tp"),
            P(None, "tp"),
            P("tp"),
            P(),
            P(),
            P("tp"),
            P("tp"),
            P("tp"),
            P("tp"),
            P("fsdp", "tp"),
        ),
        check_vma=False,
    )
```

```python
import functools

import jax
import jax.numpy as jnp
from jax import lax
from jax.experimental import pallas as pl
from jax.experimental.pallas import tpu as pltpu
from jax.sharding import PartitionSpec as P

HEADDIM = 64
NSTATE = 128
CONV = 4
SCAN_BLOCK = 256
LEN = 512
INNER = 1536


epsilon = 1e-05
highest = lax.Precision.HIGHEST
DT_PAD = 128


def causal_conv(series, kernel, offset_bias):
    length = series.shape[1]
    padded = jnp.pad(series, ((0, 0), (CONV - 1, 0), (0, 0)))
    summed = jnp.zeros(series.shape, jnp.float32) + offset_bias
    for shift_pos in range(CONV):
        summed = summed + kernel[shift_pos] * padded[:, shift_pos : shift_pos + length]
    return jax.nn.silu(summed)


def ssd_scan(values_in, delta, rates, b_proj, c_proj):
    seq_count, length, head_count, head_size = values_in.shape
    block_total = length // SCAN_BLOCK
    values = values_in.reshape(seq_count, block_total, SCAN_BLOCK, head_count, head_size)
    steps_dt = delta.reshape(seq_count, block_total, SCAN_BLOCK, head_count)
    b_blocks = b_proj.reshape(seq_count, block_total, SCAN_BLOCK, -1)
    c_blocks = c_proj.reshape(seq_count, block_total, SCAN_BLOCK, -1)
    cumulative = jnp.cumsum(steps_dt * rates, axis=2)
    by_head = jnp.transpose(cumulative, (0, 1, 3, 2))
    dt_head = jnp.transpose(steps_dt, (0, 1, 3, 2))
    places = jnp.arange(SCAN_BLOCK)
    causal = places[:, None] >= places[None, :]
    gaps = by_head[..., :, None] - by_head[..., None, :]
    weights = jnp.exp(jnp.where(causal, gaps, -1e30))
    scores = jnp.einsum("skqn,skrn->skqr", c_blocks, b_blocks, precision=highest)
    mixing = scores[:, :, None] * weights * dt_head[..., None, :]
    within = jnp.einsum("skhqr,skrhp->skqhp", mixing, values, precision=highest)
    to_end = jnp.exp(cumulative[:, :, -1:, :] - cumulative) * steps_dt
    block_states = jnp.einsum("skrh,skrhp,skrn->skhpn", to_end, values, b_blocks, precision=highest)
    fading = jnp.exp(cumulative[:, :, -1, :])
    running = jnp.zeros(block_states.shape[:1] + block_states.shape[2:], jnp.float32)
    entering = []
    for block_pos in range(block_total):
        entering.append(running)
        running = running * fading[:, block_pos, :, None, None] + block_states[:, block_pos]
    entering = jnp.stack(entering, 1)
    across = (
        jnp.einsum("skqn,skhpn->skqhp", c_blocks, entering, precision=highest)
        * jnp.exp(cumulative)[..., None]
    )
    return (within + across).reshape(seq_count, length, head_count, head_size)


def prenorm(row_block, norm_gain):
    inverse = lax.rsqrt(jnp.mean(row_block * row_block, -1, keepdims=True) + epsilon)
    return row_block * inverse * norm_gain


def conv_piece(x_raw, bc_raw, x_kernel, x_bias, bc_kernel, bc_bias):
    seq_count = x_raw.shape[0] // LEN
    x_conv = causal_conv(x_raw.reshape(seq_count, LEN, -1), x_kernel, x_bias)
    bc_conv = causal_conv(bc_raw.reshape(seq_count, LEN, -1), bc_kernel, bc_bias)
    return (x_conv.reshape(x_raw.shape), bc_conv.reshape(bc_raw.shape))


def mixer_piece(x_conv, bc_conv, dt_raw, gate_raw, dt_bias, decay_log, skip_gain):
    row_count = x_conv.shape[0]
    seq_count = row_count // LEN
    head_count = dt_raw.shape[1]
    heads_in = x_conv.reshape(seq_count, LEN, head_count, HEADDIM)
    delta = jax.nn.softplus(dt_raw.reshape(seq_count, LEN, head_count) + dt_bias)
    bc_seq = bc_conv.reshape(seq_count, LEN, 2 * NSTATE)
    result = ssd_scan(
        heads_in, delta, -jnp.exp(decay_log), bc_seq[..., :NSTATE], bc_seq[..., NSTATE:]
    )
    result = result + skip_gain[:, None] * heads_in
    return result.reshape(row_count, -1) * jax.nn.silu(gate_raw)


def rounded(value):
    return lax.optimization_barrier(value.astype(jnp.bfloat16)).astype(jnp.float32)


def contract_rows(left, right):
    return lax.dot_general(
        left, right, (((0,), (0,)), ((), ())), preferred_element_type=jnp.float32
    )


def contract_cols(left, right):
    return lax.dot_general(
        left, right, (((1,), (1,)), ((), ())), preferred_element_type=jnp.float32
    )


def project(rows_in, matrix):
    return jnp.dot(rows_in, matrix, preferred_element_type=jnp.float32).astype(jnp.bfloat16)


def local(
    tokens,
    norm_gain,
    z_weight,
    x_weight,
    bc_weight,
    dt_weight,
    x_kernel,
    x_bias,
    bc_kernel,
    bc_bias,
    dt_bias,
    decay_log,
    skip_gain,
    out_gain,
    out_weight,
    cotangent,
):
    residual = tokens.astype(jnp.float32)
    normed, norm_pull = jax.vjp(prenorm, residual, norm_gain)
    normed_low = normed.astype(jnp.bfloat16)
    full_rows = lax.all_gather(normed_low, "tp", axis=0, tiled=True)
    gathered = (
        lax.all_gather(z_weight, "fsdp", axis=0, tiled=True),
        lax.all_gather(x_weight, "fsdp", axis=0, tiled=True),
        lax.all_gather(bc_weight, "fsdp", axis=0, tiled=True),
        lax.all_gather(dt_weight, "fsdp", axis=0, tiled=True),
        lax.all_gather(out_weight, "fsdp", axis=0, tiled=True),
    )
    z_full, x_full, bc_full, dt_full, out_full = gathered
    gate_low = project(full_rows, z_full)
    xraw_low = project(full_rows, x_full)
    bcraw_low = project(full_rows, bc_full)
    dtraw_low = project(full_rows, dt_full)
    (x_conv, bc_conv), conv_pull = jax.vjp(
        conv_piece,
        xraw_low.astype(jnp.float32),
        bcraw_low.astype(jnp.float32),
        x_kernel,
        x_bias,
        bc_kernel,
        bc_bias,
    )
    x_round = rounded(x_conv)
    bc_round = rounded(bc_conv)
    gated, mixer_pull = jax.vjp(
        mixer_piece,
        x_round,
        bc_round,
        dtraw_low.astype(jnp.float32),
        gate_low.astype(jnp.float32),
        dt_bias,
        decay_log,
        skip_gain,
    )
    square_part = jnp.sum(gated * gated, -1)
    square_sum = lax.psum(square_part, "tp")
    scale = lax.rsqrt(square_sum / INNER + epsilon)[:, None]
    mixed_low = (gated * scale * out_gain).astype(jnp.bfloat16)
    branch = contract_cols(mixed_low, out_full)
    branch_rows = lax.psum_scatter(branch, "tp", scatter_dimension=0, tiled=True)
    output = (residual + branch_rows).astype(jnp.bfloat16)
    cot_rows = lax.all_gather(cotangent, "tp", axis=0, tiled=True)
    d_out_weight = contract_rows(cot_rows, mixed_low)
    d_mixed = jnp.dot(cot_rows, out_full, preferred_element_type=jnp.float32)
    d_out_gain = jnp.sum(d_mixed * gated * scale, 0)
    scaled_grad = d_mixed * out_gain
    cross_part = jnp.sum(scaled_grad * gated, -1)
    cross_sum = lax.psum(cross_part, "tp")
    d_gated = scale * scaled_grad - gated * scale**3 * (cross_sum / INNER)[:, None]
    d_x_round, d_bc_part, d_dt_raw, d_gate_raw, d_dt_bias, d_decay_log, d_skip_gain = mixer_pull(
        d_gated
    )
    d_bc_round = lax.psum(d_bc_part, "tp")
    d_x_raw, d_bc_raw, d_x_kernel, d_x_bias, d_bc_kernel, d_bc_bias = conv_pull(
        (d_x_round, d_bc_round)
    )
    gate_grad = d_gate_raw.astype(jnp.bfloat16)
    xraw_grad = d_x_raw.astype(jnp.bfloat16)
    bcraw_grad = d_bc_raw.astype(jnp.bfloat16)
    dtraw_grad = d_dt_raw.astype(jnp.bfloat16)
    d_z_weight = contract_rows(full_rows, gate_grad)
    d_x_weight = contract_rows(full_rows, xraw_grad)
    d_bc_weight = contract_rows(full_rows, bcraw_grad)
    d_dt_weight = contract_rows(full_rows, dtraw_grad)
    input_part = contract_cols(gate_grad, z_full) + contract_cols(xraw_grad, x_full)
    input_part = input_part + contract_cols(dtraw_grad, dt_full)
    input_rows = lax.psum_scatter(input_part, "tp", scatter_dimension=0, tiled=True)
    own_count = tokens.shape[0]
    own_bc = lax.dynamic_slice_in_dim(bcraw_grad, lax.axis_index("tp") * own_count, own_count, 0)
    d_normed = input_rows + contract_cols(own_bc, bc_full)
    d_residual, d_norm_part = norm_pull(d_normed)
    d_tokens = (cotangent.astype(jnp.float32) + d_residual).astype(jnp.bfloat16)
    d_z_weight, d_x_weight, d_bc_weight, d_dt_weight, d_out_weight = (
        lax.psum_scatter(d_z_weight, "fsdp", scatter_dimension=0, tiled=True),
        lax.psum_scatter(d_x_weight, "fsdp", scatter_dimension=0, tiled=True),
        lax.psum_scatter(d_bc_weight, "fsdp", scatter_dimension=0, tiled=True),
        lax.psum_scatter(d_dt_weight, "fsdp", scatter_dimension=0, tiled=True),
        lax.psum_scatter(d_out_weight, "fsdp", scatter_dimension=0, tiled=True),
    )
    (
        d_x_kernel,
        d_x_bias,
        d_bc_kernel,
        d_bc_bias,
        d_dt_bias,
        d_decay_log,
        d_skip_gain,
        d_out_gain,
    ) = lax.psum(
        (
            d_x_kernel,
            d_x_bias,
            d_bc_kernel,
            d_bc_bias,
            d_dt_bias,
            d_decay_log,
            d_skip_gain,
            d_out_gain,
        ),
        "fsdp",
    )
    d_norm_gain = lax.psum(d_norm_part, ("fsdp", "tp"))
    return (
        output,
        d_tokens,
        d_norm_gain,
        d_z_weight,
        d_x_weight,
        d_bc_weight,
        d_dt_weight,
        d_x_kernel,
        d_x_bias,
        d_bc_kernel,
        d_bc_bias,
        d_dt_bias,
        d_decay_log,
        d_skip_gain,
        d_out_gain,
        d_out_weight,
    )


def bits_of(count):
    return [1 << k for k in range(count.bit_length() - 1)]


def orders_of(fsdp_count, tp_count):
    own = bits_of(fsdp_count)
    other = [bit * fsdp_count for bit in bits_of(tp_count)]
    return (own[:2] + other + own[2:], own[:1] + other + own[1:])


def flipped(mask, fsdp_count, f_pos, t_pos):
    low, high = mask % fsdp_count, mask // fsdp_count
    for bit in bits_of(fsdp_count):
        if low & bit:
            f_pos = f_pos + bit - 2 * bit * ((lax.axis_index("fsdp") // bit) % 2)
    bit = 1
    while bit <= high:
        if high & bit:
            t_pos = t_pos + bit - 2 * bit * ((lax.axis_index("tp") // bit) % 2)
        bit *= 2
    return f_pos, t_pos


def greet(all_bits, place):
    barrier = pltpu.get_barrier_semaphore()
    for bit in all_bits:
        pl.semaphore_signal(
            barrier, inc=1, device_id=place(bit), device_id_type=pl.DeviceIdType.MESH
        )
    pl.semaphore_wait(barrier, len(all_bits))


def gather_kernel(
    fsdp_count, tp_count, shard, small, full, small_full, send_sem, recv_sem, near_sem,
    small_send, small_recv,
):
    f_own, t_own = lax.axis_index("fsdp"), lax.axis_index("tp")
    place = lambda mask: flipped(mask, fsdp_count, f_own, t_own)

    def slot(mask):
        f_pos, t_pos = place(mask)
        return t_pos * fsdp_count + f_pos

    total = fsdp_count * tp_count
    forward = orders_of(fsdp_count, tp_count)
    greet(forward[0], place)
    half = shard.shape[1] // 2
    pending = []

    def send(lane, mask, bit):
        cols = pl.ds(lane * half, half)
        source = shard.at[:, cols] if mask == 0 else full.at[slot(mask), :, cols]
        copy = pltpu.make_async_remote_copy(
            src_ref=source,
            dst_ref=full.at[slot(mask), :, cols],
            send_sem=send_sem.at[lane, mask + bit],
            recv_sem=recv_sem.at[lane, mask + bit],
            device_id=place(bit),
            device_id_type=pl.DeviceIdType.MESH,
        )
        copy.start()
        pending.append(copy)
        return copy

    arriving = {}
    orders = [list(reversed(order)) for order in forward]
    for lane in range(2):
        for bit in orders[lane]:
            arriving[lane, bit] = send(lane, 0, bit)
    near = pltpu.make_async_copy(shard, full.at[slot(0)], near_sem.at[0])
    near.start()
    near_small = pltpu.make_async_copy(small, small_full.at[t_own], near_sem.at[1])
    near_small.start()
    small_copies = []
    for t_mask in range(1, tp_count):
        copy = pltpu.make_async_remote_copy(
            src_ref=small,
            dst_ref=small_full.at[t_own],
            send_sem=small_send.at[t_mask],
            recv_sem=small_recv.at[t_mask],
            device_id=place(t_mask * fsdp_count),
            device_id_type=pl.DeviceIdType.MESH,
        )
        copy.start()
        small_copies.append(copy)
    held = [[0], [0]]
    for stage in range(len(forward[0])):
        for lane in range(2):
            bit = orders[lane][stage]
            later = orders[lane][stage + 1 :]
            for mask in list(held[lane]):
                arriving[lane, mask + bit].wait_recv()
                held[lane].append(mask + bit)
                for next_bit in later:
                    arriving[lane, mask + bit + next_bit] = send(lane, mask + bit, next_bit)
    for copy in small_copies:
        copy.wait()
    for copy in pending:
        copy.wait_send()
    near.wait()
    near_small.wait()


def gather_all(shard, small, fsdp_count, tp_count):
    total = fsdp_count * tp_count
    return pl.pallas_call(
        functools.partial(gather_kernel, fsdp_count, tp_count),
        out_shape=(
            jax.ShapeDtypeStruct((total,) + shard.shape, shard.dtype),
            jax.ShapeDtypeStruct((tp_count,) + small.shape, small.dtype),
        ),
        in_specs=[pl.BlockSpec(memory_space=pltpu.VMEM)] * 2,
        out_specs=(pl.BlockSpec(memory_space=pltpu.VMEM),) * 2,
        scratch_shapes=[
            pltpu.SemaphoreType.DMA((2, total)),
            pltpu.SemaphoreType.DMA((2, total)),
            pltpu.SemaphoreType.DMA((2,)),
            pltpu.SemaphoreType.DMA((tp_count,)),
            pltpu.SemaphoreType.DMA((tp_count,)),
        ],
        compiler_params=pltpu.CompilerParams(
            collective_id=0, has_side_effects=True, vmem_limit_bytes=40 << 20
        ),
        name="gather_weights",
    )(shard, small)


def reduce_kernel(
    fsdp_count, tp_count, lanes, first, second, small, first_out, second_out, small_out,
    first_got, second_got, first_sum, second_sum, small_sum, small_got,
    send_sem, recv_sem, small_send, small_recv,
):
    f_own, t_own = lax.axis_index("fsdp"), lax.axis_index("tp")
    place = lambda mask: flipped(mask, fsdp_count, f_own, t_own)

    def slot(mask):
        f_pos, t_pos = place(mask)
        return t_pos * fsdp_count + f_pos

    total = fsdp_count * tp_count
    both = orders_of(fsdp_count, tp_count)
    greet(both[0], place)
    parts = ((first, first_got, first_sum, first_out), (second, second_got, second_sum, second_out))
    stages = len(both[0])
    pending = []
    arriving = {}
    small_copies = []
    for stage in range(stages + 1):
        if stage < stages:
            bit = both[0][stage]
            source = small if stage == 0 else small_sum.at[stage - 1]
            small_copy = pltpu.make_async_remote_copy(
                src_ref=source,
                dst_ref=small_got.at[stage],
                send_sem=small_send.at[stage],
                recv_sem=small_recv.at[stage],
                device_id=place(bit),
                device_id_type=pl.DeviceIdType.MESH,
            )
            small_copy.start()
            pending.append(small_copy)
        for lane, (which, start, size, order_pos) in enumerate(lanes):
            given, got, held, out = parts[which]
            order = both[order_pos]
            cols = pl.ds(start, size)
            kept = [m for m in range(total) if not any(m & b for b in order[:stage])]
            if stage > 0:
                previous = order[stage - 1]
                now = order[stage] if stage < stages else 0
                kept = sorted(kept, key=lambda m: not (m & now))
            for mask in kept:
                if stage > 0:
                    arriving[lane, mask + previous].wait_recv()
                    before = given[slot(mask), :, cols] if stage == 1 else held[mask // 2, :, cols]
                    add = got[mask + previous, :, cols]
                    if stage == stages:
                        out[:, cols] = before.astype(jnp.float32) + add.astype(jnp.float32)
                    else:
                        held[mask // 2, :, cols] = before + add
                if stage < stages and mask & order[stage]:
                    source = (
                        given.at[slot(mask), :, cols]
                        if stage == 0
                        else held.at[mask // 2, :, cols]
                    )
                    copy = pltpu.make_async_remote_copy(
                        src_ref=source,
                        dst_ref=got.at[mask, :, cols],
                        send_sem=send_sem.at[lane, mask],
                        recv_sem=recv_sem.at[lane, mask],
                        device_id=place(order[stage]),
                        device_id_type=pl.DeviceIdType.MESH,
                    )
                    copy.start()
                    pending.append(copy)
                    arriving[lane, mask] = copy
        if stage < stages:
            small_copy.wait_recv()
            before = small[...] if stage == 0 else small_sum[stage - 1]
            if stage == stages - 1:
                small_out[...] = before + small_got[stage]
            else:
                small_sum[stage] = before + small_got[stage]
    for copy in pending:
        copy.wait_send()


def reduce_all(first, second, small, fsdp_count, tp_count):
    total, rows, wide = first.shape
    narrow = second.shape[2]
    cut = (wide * 3 // 5) // 128 * 128
    lanes = ((1, 0, narrow, 0), (0, 0, cut, 1), (0, cut, wide - cut, 0))
    stages = total.bit_length() - 1
    low = jnp.bfloat16
    return pl.pallas_call(
        functools.partial(reduce_kernel, fsdp_count, tp_count, lanes),
        out_shape=(
            jax.ShapeDtypeStruct((rows, wide), jnp.float32),
            jax.ShapeDtypeStruct((rows, narrow), jnp.float32),
            jax.ShapeDtypeStruct(small.shape, jnp.float32),
        ),
        in_specs=[pl.BlockSpec(memory_space=pltpu.VMEM)] * 3,
        out_specs=(pl.BlockSpec(memory_space=pltpu.VMEM),) * 3,
        scratch_shapes=[
            pltpu.VMEM((total, rows, wide), low),
            pltpu.VMEM((total, rows, narrow), low),
            pltpu.VMEM((total // 2, rows, wide), low),
            pltpu.VMEM((total // 2, rows, narrow), low),
            pltpu.VMEM((stages,) + small.shape, jnp.float32),
            pltpu.VMEM((stages,) + small.shape, jnp.float32),
            pltpu.SemaphoreType.DMA((len(lanes), total)),
            pltpu.SemaphoreType.DMA((len(lanes), total)),
            pltpu.SemaphoreType.DMA((stages,)),
            pltpu.SemaphoreType.DMA((stages,)),
        ],
        compiler_params=pltpu.CompilerParams(
            collective_id=1, has_side_effects=True, vmem_limit_bytes=48 << 20
        ),
        name="reduce_gradients",
    )(first, second, small)


def pad_cols(value, width):
    return jnp.pad(value, ((0, 0), (0, width - value.shape[1])))


def by_sequence(
    fsdp_count,
    tp_count,
    tokens,
    norm_gain,
    z_weight,
    x_weight,
    bc_weight,
    dt_weight,
    x_kernel,
    x_bias,
    bc_kernel,
    bc_bias,
    dt_bias,
    decay_log,
    skip_gain,
    out_gain,
    out_weight,
    cotangent,
):
    rows, width = z_weight.shape
    heads = dt_weight.shape[1]
    depth = tokens.shape[1]
    count = tokens.shape[0]
    bc_share = 2 * NSTATE // tp_count
    bc_own = lax.dynamic_slice_in_dim(bc_weight, lax.axis_index("tp") * bc_share, bc_share, 1)
    shard = jnp.concatenate(
        [z_weight, x_weight, pad_cols(dt_weight, DT_PAD), bc_own, out_weight], 1
    )
    small = jnp.concatenate(
        [
            x_kernel,
            x_bias[None],
            out_gain[None],
            pad_cols(jnp.concatenate([dt_bias, decay_log, skip_gain])[None], width),
            jnp.zeros((1, width), jnp.float32),
        ],
        0,
    )
    full, small_full = gather_all(shard, small, fsdp_count, tp_count)
    full = full.reshape(tp_count, depth, shard.shape[1])
    out_start = 2 * width + DT_PAD + bc_share
    proj_w, out_w = full[:, :, :out_start], full[:, :, out_start:]
    join = lambda value: jnp.moveaxis(value, 0, -2).reshape(value.shape[1:-1] + (-1,))
    x_kernel_all = join(small_full[:, :CONV])
    x_bias_all = small_full[:, CONV].reshape(-1)
    out_gain_all = small_full[:, CONV + 1]
    tiny = small_full[:, CONV + 2, : 3 * heads].reshape(tp_count, 3, heads)
    dt_bias_all, decay_all, skip_all = (tiny[:, k].reshape(-1) for k in range(3))

    residual = tokens.astype(jnp.float32)
    normed, norm_pull = jax.vjp(prenorm, residual, norm_gain)
    normed_low = normed.astype(jnp.bfloat16)
    raw = jnp.einsum(
        "rk,tkc->trc", normed_low, proj_w, preferred_element_type=jnp.float32
    ).astype(jnp.bfloat16)
    gate_low = join(raw[:, :, :width])
    xraw_low = join(raw[:, :, width : 2 * width])
    dtraw_low = join(raw[:, :, 2 * width : 2 * width + heads])
    bcraw_low = join(raw[:, :, 2 * width + DT_PAD :])
    gated, scan_pull, conv_pull = mixer(
        xraw_low, bcraw_low, dtraw_low, gate_low, x_kernel_all, x_bias_all, bc_kernel, bc_bias,
        dt_bias_all, decay_all, skip_all,
    )
    scale = lax.rsqrt(jnp.sum(gated * gated, -1) / INNER + epsilon)[:, None]
    gain = out_gain_all.reshape(-1)
    mixed_low = (gated * scale * gain).astype(jnp.bfloat16)
    split = lambda value: jnp.moveaxis(value.reshape(value.shape[0], tp_count, -1), 1, 0)
    mixed_split = split(mixed_low)
    branch = jnp.einsum("trc,tkc->rk", mixed_split, out_w, preferred_element_type=jnp.float32)
    output = (residual + branch).astype(jnp.bfloat16)
    d_out_weight = jnp.einsum(
        "rk,trc->tkc", cotangent, mixed_split, preferred_element_type=jnp.float32
    ).astype(jnp.bfloat16)
    d_mixed = jnp.einsum("rk,tkc->trc", cotangent, out_w, preferred_element_type=jnp.float32)
    d_mixed = join(d_mixed)
    d_out_gain = jnp.sum(d_mixed * gated * scale, 0)
    scaled_grad = d_mixed * gain
    cross_sum = jnp.sum(scaled_grad * gated, -1)
    d_gated = scale * scaled_grad - gated * scale**3 * (cross_sum / INNER)[:, None]
    d_x_round, d_bc_round, d_dt_raw, d_gate_raw, d_dt_bias, d_decay_log, d_skip_gain = scan_pull(
        d_gated
    )
    d_x_raw, d_bc_raw, d_x_kernel, d_x_bias, d_bc_kernel, d_bc_bias = conv_pull(
        (d_x_round, d_bc_round)
    )
    low = jnp.bfloat16
    bc_grad = d_bc_raw.astype(low)
    dt_grad = split(d_dt_raw.astype(low))
    dt_grad = jnp.pad(dt_grad, ((0, 0), (0, 0), (0, DT_PAD - heads)))
    lead = jnp.concatenate([split(d_gate_raw.astype(low)), split(d_x_raw.astype(low)), dt_grad], 2)
    proj_grad = jnp.concatenate([lead, split(bc_grad)], 2)
    d_normed = jnp.einsum("trc,tkc->rk", proj_grad, proj_w, preferred_element_type=jnp.float32)
    bc_all = jnp.broadcast_to(bc_grad[None], (tp_count,) + bc_grad.shape)
    d_proj = jnp.einsum(
        "rk,trc->tkc",
        normed_low,
        jnp.concatenate([lead, bc_all], 2),
        preferred_element_type=jnp.float32,
    ).astype(low)
    d_residual, d_norm_gain = norm_pull(d_normed)
    d_tokens = (cotangent.astype(jnp.float32) + d_residual).astype(jnp.bfloat16)
    tiny_grad = jnp.stack([d_dt_bias, d_decay_log, d_skip_gain]).reshape(3, tp_count, heads)
    tiny_grad = jnp.moveaxis(tiny_grad, 1, 0).reshape(tp_count, 3 * heads)
    flat = jnp.concatenate(
        [
            d_norm_gain,
            d_bc_kernel.reshape(-1),
            d_bc_bias,
            d_out_gain,
            d_x_bias,
            d_x_kernel.reshape(-1),
            tiny_grad.reshape(-1),
        ]
    )
    lines = -(-flat.size // width)
    lines = -(-lines // 8) * 8
    small_grad = jnp.pad(flat, (0, lines * width - flat.size)).reshape(lines, width)
    wide, narrow, sums = reduce_all(
        d_proj.reshape(fsdp_count * tp_count, rows, -1),
        d_out_weight.reshape(fsdp_count * tp_count, rows, -1),
        small_grad,
        fsdp_count,
        tp_count,
    )
    sums = sums.reshape(-1)
    t_own = lax.axis_index("tp")
    position = 0

    def take(*shape):
        nonlocal position
        size = 1
        for extent in shape:
            size *= extent
        piece = sums[position : position + size].reshape(shape)
        position += size
        return piece

    own = lambda value: lax.dynamic_index_in_dim(value, t_own, value.ndim - 2, keepdims=False)
    d_norm_gain = take(depth)
    d_bc_kernel = take(CONV, 2 * NSTATE)
    d_bc_bias = take(2 * NSTATE)
    d_out_gain = own(take(tp_count, width))
    d_x_bias = own(take(tp_count, width))
    d_x_kernel = own(take(CONV, tp_count, width))
    d_tiny = own(take(tp_count, 3 * heads)).reshape(3, heads)
    return (
        output,
        d_tokens,
        d_norm_gain,
        wide[:, :width],
        wide[:, width : 2 * width],
        wide[:, 2 * width + DT_PAD :],
        wide[:, 2 * width : 2 * width + heads],
        d_x_kernel,
        d_x_bias,
        d_bc_kernel,
        d_bc_bias,
        d_tiny[0],
        d_tiny[1],
        d_tiny[2],
        d_out_gain,
        narrow,
    )


def pair_parts(x_ref, cum_ref, cum_row_ref, dt_ref, b_ref, c_ref, scores):
    size = SCAN_BLOCK
    lane = lax.broadcasted_iota(jnp.int32, (size, 2 * HEADDIM), 1)
    left = lane < HEADDIM
    causal = lax.broadcasted_iota(jnp.int32, (size, size), 0) >= lax.broadcasted_iota(
        jnp.int32, (size, size), 1
    )
    spread = lambda pair: jnp.where(left, pair[:, 0:1], pair[:, 1:2])
    parts = []
    for block in range(2):
        rows = slice(block * size, (block + 1) * size)
        cum, dt = cum_ref[0, rows], dt_ref[0, rows]
        x = x_ref[rows].astype(jnp.float32)
        scaled = x * spread(dt)
        masks, mixes = [], []
        for head in range(2):
            gaps = cum[:, head : head + 1] - cum_row_ref[0, head : head + 1, rows]
            mask = jnp.exp(jnp.where(causal, gaps, -1e30))
            masks.append(mask)
            mixes.append(scores[block] * mask)
        parts.append((rows, cum, dt, x, scaled, masks, mixes))
    return left, spread, parts


def dot_of(left, right, left_dim, right_dim):
    low = jnp.bfloat16
    return lax.dot_general(
        left.astype(low),
        right.astype(low),
        (((left_dim,), (right_dim,)), ((), ())),
        preferred_element_type=jnp.float32,
    )


def head_outputs(left, spread, parts, b_ref, c_ref):
    found = []
    for rows, cum, dt, x, scaled, masks, mixes in parts:
        found.append(
            dot_of(mixes[0], jnp.where(left, scaled, 0.0), 1, 0)
            + dot_of(mixes[1], jnp.where(left, 0.0, scaled), 1, 0)
        )
    rows, cum, dt, x, scaled, masks, mixes = parts[0]
    to_end = jnp.exp(spread(cum[SCAN_BLOCK - 1 : SCAN_BLOCK] - cum))
    ended = to_end * scaled
    state = dot_of(b_ref[rows], ended, 0, 0)
    later = parts[1][0]
    growth = jnp.exp(spread(parts[1][1]))
    across = growth * dot_of(c_ref[later], state, 1, 0)
    found[1] = found[1] + across
    return found, state, to_end, ended, growth, across


def fill_scores(scores, b_ref, c_ref):
    for block in range(2):
        rows = slice(block * SCAN_BLOCK, (block + 1) * SCAN_BLOCK)
        scores[block] = dot_of(c_ref[rows], b_ref[rows], 1, 1)


def scan_forward(
    x_ref, gate_ref, b_ref, c_ref, cum_ref, cum_row_ref, dt_ref, skip_ref, gated_ref, scores
):
    @pl.when(pl.program_id(0) == 0)
    def _():
        fill_scores(scores, b_ref, c_ref)

    left, spread, parts = pair_parts(x_ref, cum_ref, cum_row_ref, dt_ref, b_ref, c_ref, scores)
    found = head_outputs(left, spread, parts, b_ref, c_ref)[0]
    for block in range(2):
        rows, x = parts[block][0], parts[block][3]
        gate = gate_ref[rows].astype(jnp.float32)
        gated_ref[rows] = (found[block] + skip_ref[0] * x) * (gate / (1.0 + jnp.exp(-gate)))


def scan_backward(
    x_ref, gate_ref, b_ref, c_ref, cum_ref, cum_row_ref, dt_ref, skip_ref, grad_ref,
    d_x_ref, d_gate_ref, d_b_ref, d_c_ref, d_cols_ref, d_row_ref, d_skip_ref,
    scores, d_scores,
):
    step = pl.program_id(0)

    @pl.when(step == 0)
    def _():
        fill_scores(scores, b_ref, c_ref)
        d_scores[...] = jnp.zeros_like(d_scores)
        d_b_ref[...] = jnp.zeros_like(d_b_ref)
        d_c_ref[...] = jnp.zeros_like(d_c_ref)

    left, spread, parts = pair_parts(x_ref, cum_ref, cum_row_ref, dt_ref, b_ref, c_ref, scores)
    found, state, to_end, ended, growth, across = head_outputs(left, spread, parts, b_ref, c_ref)
    skip = skip_ref[0]
    grads, d_scaled, d_cum = [], [], []
    d_skip = jnp.zeros((1, 2 * HEADDIM), jnp.float32)

    def per_head(value):
        return (
            jnp.sum(jnp.where(left, value, 0.0), 1, keepdims=True),
            jnp.sum(jnp.where(left, 0.0, value), 1, keepdims=True),
        )

    for block in range(2):
        rows, cum, dt, x, scaled, masks, mixes = parts[block]
        gate = gate_ref[rows].astype(jnp.float32)
        sigmoid = 1.0 / (1.0 + jnp.exp(-gate))
        outer = grad_ref[rows]
        inner = found[block] + skip * x
        d_gate = outer * inner * sigmoid * (1.0 + gate * (1.0 - sigmoid))
        d_gate_ref[rows] = d_gate.astype(d_gate_ref.dtype)
        grad = outer * gate * sigmoid
        d_skip = d_skip + jnp.sum(grad * x, 0, keepdims=True)
        halves = (jnp.where(left, grad, 0.0), jnp.where(left, 0.0, grad))
        back = jnp.zeros_like(grad)
        sums = []
        total = jnp.zeros((SCAN_BLOCK, SCAN_BLOCK), jnp.float32)
        for head in range(2):
            d_mix = dot_of(halves[head], scaled, 1, 1)
            total = total + d_mix * masks[head]
            both = d_mix * mixes[head]
            sums.append(jnp.sum(both, 1, keepdims=True))
            d_row_ref[0, head : head + 1, rows] = jnp.sum(both, 0, keepdims=True)
            back = back + dot_of(mixes[head], halves[head], 0, 0)
        d_scores[block] += total
        grads.append(grad)
        d_scaled.append(back)
        d_cum.append(sums)
    later, early = parts[1][0], parts[0][0]
    d_across = grads[1] * growth
    d_c_ref[later] += dot_of(d_across, state, 1, 1)
    d_state = dot_of(c_ref[later], d_across, 0, 0)
    extra = per_head(grads[1] * across)
    d_cum[1] = [d_cum[1][head] + extra[head] for head in range(2)]
    d_ended = dot_of(b_ref[early], d_state, 1, 0)
    d_b_ref[early] += dot_of(ended, d_state, 1, 1)
    d_scaled[0] = d_scaled[0] + d_ended * to_end
    decayed = per_head(d_ended * ended)
    last = lax.broadcasted_iota(jnp.int32, (SCAN_BLOCK, 1), 0) == SCAN_BLOCK - 1
    d_cum[0] = [
        d_cum[0][head]
        - decayed[head]
        + jnp.where(last, jnp.sum(decayed[head], 0, keepdims=True), 0.0)
        for head in range(2)
    ]
    spot = lax.broadcasted_iota(jnp.int32, (SCAN_BLOCK, 4), 1)
    for block in range(2):
        rows, cum, dt, x, scaled, masks, mixes = parts[block]
        d_x_ref[rows] = d_scaled[block] * spread(dt) + skip * grads[block]
        d_dt = per_head(d_scaled[block] * x)
        d_cols_ref[0, rows] = jnp.where(
            spot < 2,
            jnp.where(spot == 0, d_cum[block][0], d_cum[block][1]),
            jnp.where(spot == 2, d_dt[0], d_dt[1]),
        )
    d_skip_ref[0] = d_skip

    @pl.when(step == pl.num_programs(0) - 1)
    def _():
        for block in range(2):
            rows = slice(block * SCAN_BLOCK, (block + 1) * SCAN_BLOCK)
            d_c_ref[rows] += dot_of(d_scores[block], b_ref[rows], 1, 0)
            d_b_ref[rows] += dot_of(d_scores[block], c_ref[rows], 0, 0)


def steps_of(dt_raw, dt_bias, decay_log):
    delta = jax.nn.softplus(dt_raw + dt_bias)
    places = jnp.arange(SCAN_BLOCK)
    causal = (places[:, None] >= places[None, :]).astype(jnp.float32)
    steps = (delta * -jnp.exp(decay_log)).reshape(-1, SCAN_BLOCK, delta.shape[1])
    cum = jnp.einsum("qr,krh->kqh", causal, steps, precision=highest)
    return delta, cum.reshape(delta.shape)


def mixer_by_pairs(x_conv, bc_conv, dt_raw, gate, dt_bias, decay_log, skip_gain):
    count, channels = x_conv.shape
    pairs = channels // (2 * HEADDIM)
    (delta, cum), steps_pull = jax.vjp(steps_of, dt_raw.astype(jnp.float32), dt_bias, decay_log)
    paired = lambda value: jnp.moveaxis(value.reshape(count, pairs, 2), 1, 0)
    skip = jnp.repeat(skip_gain, HEADDIM).reshape(pairs, 1, 2 * HEADDIM)
    cum_col = paired(cum)
    given = (
        x_conv, gate, bc_conv, bc_conv, cum_col, jnp.swapaxes(cum_col, 1, 2), paired(delta), skip,
    )
    own = pl.BlockSpec((count, 2 * HEADDIM), lambda j: (0, j))
    whole = lambda place: pl.BlockSpec((count, NSTATE), lambda j: (0, place))
    column = pl.BlockSpec((1, count, 2), lambda j: (j, 0, 0))
    line = pl.BlockSpec((1, 2, count), lambda j: (j, 0, 0))
    single = pl.BlockSpec((1, 1, 2 * HEADDIM), lambda j: (j, 0, 0))
    specs = [own, own, whole(0), whole(1), column, line, column, single]
    square = pltpu.VMEM((2, SCAN_BLOCK, SCAN_BLOCK), jnp.float32)
    params = pltpu.CompilerParams(vmem_limit_bytes=32 << 20)
    full = jax.ShapeDtypeStruct
    gated = pl.pallas_call(
        scan_forward,
        grid=(pairs,),
        in_specs=specs,
        out_specs=own,
        out_shape=full((count, channels), jnp.float32),
        scratch_shapes=[square],
        compiler_params=params,
        name="scan_forward",
    )(*given)

    def pull(d_gated):
        d_x, d_gate, d_b, d_c, d_cols, d_row, d_skip = pl.pallas_call(
            scan_backward,
            grid=(pairs,),
            in_specs=specs + [own],
            out_specs=(
                own, own, whole(0), whole(0), pl.BlockSpec((1, count, 4), lambda j: (j, 0, 0)),
                line, single,
            ),
            out_shape=(
                full((count, channels), jnp.float32),
                full((count, channels), jnp.bfloat16),
                full((count, NSTATE), jnp.float32),
                full((count, NSTATE), jnp.float32),
                full((pairs, count, 4), jnp.float32),
                full((pairs, 2, count), jnp.float32),
                full((pairs, 1, 2 * HEADDIM), jnp.float32),
            ),
            scratch_shapes=[square, square],
            compiler_params=params,
            name="scan_backward",
        )(*given, d_gated)
        merged = lambda value: jnp.moveaxis(value, 0, 1).reshape(count, 2 * pairs)
        d_cum = merged(d_cols[:, :, :2] - jnp.swapaxes(d_row, 1, 2))
        d_dt_raw, d_dt_bias, d_decay_log = steps_pull((merged(d_cols[:, :, 2:]), d_cum))
        d_skip_gain = jnp.sum(d_skip.reshape(2 * pairs, HEADDIM), 1)
        return (
            d_x, jnp.concatenate([d_b, d_c], 1), d_dt_raw, d_gate, d_dt_bias, d_decay_log,
            d_skip_gain,
        )

    return gated, pull


def mixer(
    xraw_low, bcraw_low, dtraw_low, gate_low, x_kernel, x_bias, bc_kernel, bc_bias, dt_bias,
    decay_log, skip_gain,
):
    (x_conv, bc_conv), conv_pull = jax.vjp(
        conv_piece,
        xraw_low.astype(jnp.float32),
        bcraw_low.astype(jnp.float32),
        x_kernel,
        x_bias,
        bc_kernel,
        bc_bias,
    )
    low = jnp.bfloat16
    gated, scan_pull = mixer_by_pairs(
        x_conv.astype(low), bc_conv.astype(low), dtraw_low, gate_low, dt_bias, decay_log, skip_gain
    )
    return gated, scan_pull, conv_pull


def solution(mesh):
    placed = (
        P(("fsdp", "tp"), None),
        P(),
        P("fsdp", "tp"),
        P("fsdp", "tp"),
        P("fsdp", None),
        P("fsdp", "tp"),
        P(None, "tp"),
        P("tp"),
        P(),
        P(),
        P("tp"),
        P("tp"),
        P("tp"),
        P("tp"),
        P("fsdp", "tp"),
        P(("fsdp", "tp"), None),
    )
    fsdp_count, tp_count = mesh.shape["fsdp"], mesh.shape["tp"]
    total = fsdp_count * tp_count

    def program(*arrays):
        rows, width = arrays[2].shape
        whole = arrays[0].shape[0] == LEN == 2 * SCAN_BLOCK and 2 * NSTATE % (128 * tp_count) == 0
        tiled = rows % 16 == 0 and width % 128 == 0 and arrays[0].shape[1] == width
        if whole and tiled and total & (total - 1) == 0 and fsdp_count >= 4:
            return by_sequence(fsdp_count, tp_count, *arrays)
        return local(*arrays)

    return jax.shard_map(
        program,
        mesh=mesh,
        in_specs=placed,
        out_specs=(
            P(("fsdp", "tp"), None),
            P(("fsdp", "tp"), None),
            P(),
            P("fsdp", "tp"),
            P("fsdp", "tp"),
            P("fsdp", None),
            P("fsdp", "tp"),
            P(None, "tp"),
            P("tp"),
            P(),
            P(),
            P("tp"),
            P("tp"),
            P("tp"),
            P("tp"),
            P("fsdp", "tp"),
        ),
        check_vma=False,
    )
```

```python
import functools

import jax
import jax.numpy as jnp
from jax import lax
from jax.experimental import pallas as pl
from jax.experimental.pallas import tpu as pltpu
from jax.sharding import PartitionSpec as P

HEADDIM = 64
NSTATE = 128
CONV = 4
SCAN_BLOCK = 256
LEN = 512
INNER = 1536


epsilon = 1e-05
highest = lax.Precision.HIGHEST
DT_PAD = 128


def causal_conv(series, kernel, offset_bias):
    length = series.shape[1]
    padded = jnp.pad(series, ((0, 0), (CONV - 1, 0), (0, 0)))
    summed = jnp.zeros(series.shape, jnp.float32) + offset_bias
    for shift_pos in range(CONV):
        summed = summed + kernel[shift_pos] * padded[:, shift_pos : shift_pos + length]
    return jax.nn.silu(summed)


def ssd_scan(values_in, delta, rates, b_proj, c_proj):
    seq_count, length, head_count, head_size = values_in.shape
    block_total = length // SCAN_BLOCK
    values = values_in.reshape(seq_count, block_total, SCAN_BLOCK, head_count, head_size)
    steps_dt = delta.reshape(seq_count, block_total, SCAN_BLOCK, head_count)
    b_blocks = b_proj.reshape(seq_count, block_total, SCAN_BLOCK, -1)
    c_blocks = c_proj.reshape(seq_count, block_total, SCAN_BLOCK, -1)
    cumulative = jnp.cumsum(steps_dt * rates, axis=2)
    by_head = jnp.transpose(cumulative, (0, 1, 3, 2))
    dt_head = jnp.transpose(steps_dt, (0, 1, 3, 2))
    places = jnp.arange(SCAN_BLOCK)
    causal = places[:, None] >= places[None, :]
    gaps = by_head[..., :, None] - by_head[..., None, :]
    weights = jnp.exp(jnp.where(causal, gaps, -1e30))
    scores = jnp.einsum("skqn,skrn->skqr", c_blocks, b_blocks, precision=highest)
    mixing = scores[:, :, None] * weights * dt_head[..., None, :]
    within = jnp.einsum("skhqr,skrhp->skqhp", mixing, values, precision=highest)
    to_end = jnp.exp(cumulative[:, :, -1:, :] - cumulative) * steps_dt
    block_states = jnp.einsum("skrh,skrhp,skrn->skhpn", to_end, values, b_blocks, precision=highest)
    fading = jnp.exp(cumulative[:, :, -1, :])
    running = jnp.zeros(block_states.shape[:1] + block_states.shape[2:], jnp.float32)
    entering = []
    for block_pos in range(block_total):
        entering.append(running)
        running = running * fading[:, block_pos, :, None, None] + block_states[:, block_pos]
    entering = jnp.stack(entering, 1)
    across = (
        jnp.einsum("skqn,skhpn->skqhp", c_blocks, entering, precision=highest)
        * jnp.exp(cumulative)[..., None]
    )
    return (within + across).reshape(seq_count, length, head_count, head_size)


def prenorm(row_block, norm_gain):
    inverse = lax.rsqrt(jnp.mean(row_block * row_block, -1, keepdims=True) + epsilon)
    return row_block * inverse * norm_gain


def conv_piece(x_raw, bc_raw, x_kernel, x_bias, bc_kernel, bc_bias):
    seq_count = x_raw.shape[0] // LEN
    x_conv = causal_conv(x_raw.reshape(seq_count, LEN, -1), x_kernel, x_bias)
    bc_conv = causal_conv(bc_raw.reshape(seq_count, LEN, -1), bc_kernel, bc_bias)
    return (x_conv.reshape(x_raw.shape), bc_conv.reshape(bc_raw.shape))


def mixer_piece(x_conv, bc_conv, dt_raw, gate_raw, dt_bias, decay_log, skip_gain):
    row_count = x_conv.shape[0]
    seq_count = row_count // LEN
    head_count = dt_raw.shape[1]
    heads_in = x_conv.reshape(seq_count, LEN, head_count, HEADDIM)
    delta = jax.nn.softplus(dt_raw.reshape(seq_count, LEN, head_count) + dt_bias)
    bc_seq = bc_conv.reshape(seq_count, LEN, 2 * NSTATE)
    result = ssd_scan(
        heads_in, delta, -jnp.exp(decay_log), bc_seq[..., :NSTATE], bc_seq[..., NSTATE:]
    )
    result = result + skip_gain[:, None] * heads_in
    return result.reshape(row_count, -1) * jax.nn.silu(gate_raw)


def rounded(value):
    return lax.optimization_barrier(value.astype(jnp.bfloat16)).astype(jnp.float32)


def contract_rows(left, right):
    return lax.dot_general(
        left, right, (((0,), (0,)), ((), ())), preferred_element_type=jnp.float32
    )


def contract_cols(left, right):
    return lax.dot_general(
        left, right, (((1,), (1,)), ((), ())), preferred_element_type=jnp.float32
    )


def project(rows_in, matrix):
    return jnp.dot(rows_in, matrix, preferred_element_type=jnp.float32).astype(jnp.bfloat16)


def local(
    tokens,
    norm_gain,
    z_weight,
    x_weight,
    bc_weight,
    dt_weight,
    x_kernel,
    x_bias,
    bc_kernel,
    bc_bias,
    dt_bias,
    decay_log,
    skip_gain,
    out_gain,
    out_weight,
    cotangent,
):
    residual = tokens.astype(jnp.float32)
    normed, norm_pull = jax.vjp(prenorm, residual, norm_gain)
    normed_low = normed.astype(jnp.bfloat16)
    full_rows = lax.all_gather(normed_low, "tp", axis=0, tiled=True)
    gathered = (
        lax.all_gather(z_weight, "fsdp", axis=0, tiled=True),
        lax.all_gather(x_weight, "fsdp", axis=0, tiled=True),
        lax.all_gather(bc_weight, "fsdp", axis=0, tiled=True),
        lax.all_gather(dt_weight, "fsdp", axis=0, tiled=True),
        lax.all_gather(out_weight, "fsdp", axis=0, tiled=True),
    )
    z_full, x_full, bc_full, dt_full, out_full = gathered
    gate_low = project(full_rows, z_full)
    xraw_low = project(full_rows, x_full)
    bcraw_low = project(full_rows, bc_full)
    dtraw_low = project(full_rows, dt_full)
    (x_conv, bc_conv), conv_pull = jax.vjp(
        conv_piece,
        xraw_low.astype(jnp.float32),
        bcraw_low.astype(jnp.float32),
        x_kernel,
        x_bias,
        bc_kernel,
        bc_bias,
    )
    x_round = rounded(x_conv)
    bc_round = rounded(bc_conv)
    gated, mixer_pull = jax.vjp(
        mixer_piece,
        x_round,
        bc_round,
        dtraw_low.astype(jnp.float32),
        gate_low.astype(jnp.float32),
        dt_bias,
        decay_log,
        skip_gain,
    )
    square_part = jnp.sum(gated * gated, -1)
    square_sum = lax.psum(square_part, "tp")
    scale = lax.rsqrt(square_sum / INNER + epsilon)[:, None]
    mixed_low = (gated * scale * out_gain).astype(jnp.bfloat16)
    branch = contract_cols(mixed_low, out_full)
    branch_rows = lax.psum_scatter(branch, "tp", scatter_dimension=0, tiled=True)
    output = (residual + branch_rows).astype(jnp.bfloat16)
    cot_rows = lax.all_gather(cotangent, "tp", axis=0, tiled=True)
    d_out_weight = contract_rows(cot_rows, mixed_low)
    d_mixed = jnp.dot(cot_rows, out_full, preferred_element_type=jnp.float32)
    d_out_gain = jnp.sum(d_mixed * gated * scale, 0)
    scaled_grad = d_mixed * out_gain
    cross_part = jnp.sum(scaled_grad * gated, -1)
    cross_sum = lax.psum(cross_part, "tp")
    d_gated = scale * scaled_grad - gated * scale**3 * (cross_sum / INNER)[:, None]
    d_x_round, d_bc_part, d_dt_raw, d_gate_raw, d_dt_bias, d_decay_log, d_skip_gain = mixer_pull(
        d_gated
    )
    d_bc_round = lax.psum(d_bc_part, "tp")
    d_x_raw, d_bc_raw, d_x_kernel, d_x_bias, d_bc_kernel, d_bc_bias = conv_pull(
        (d_x_round, d_bc_round)
    )
    gate_grad = d_gate_raw.astype(jnp.bfloat16)
    xraw_grad = d_x_raw.astype(jnp.bfloat16)
    bcraw_grad = d_bc_raw.astype(jnp.bfloat16)
    dtraw_grad = d_dt_raw.astype(jnp.bfloat16)
    d_z_weight = contract_rows(full_rows, gate_grad)
    d_x_weight = contract_rows(full_rows, xraw_grad)
    d_bc_weight = contract_rows(full_rows, bcraw_grad)
    d_dt_weight = contract_rows(full_rows, dtraw_grad)
    input_part = contract_cols(gate_grad, z_full) + contract_cols(xraw_grad, x_full)
    input_part = input_part + contract_cols(dtraw_grad, dt_full)
    input_rows = lax.psum_scatter(input_part, "tp", scatter_dimension=0, tiled=True)
    own_count = tokens.shape[0]
    own_bc = lax.dynamic_slice_in_dim(bcraw_grad, lax.axis_index("tp") * own_count, own_count, 0)
    d_normed = input_rows + contract_cols(own_bc, bc_full)
    d_residual, d_norm_part = norm_pull(d_normed)
    d_tokens = (cotangent.astype(jnp.float32) + d_residual).astype(jnp.bfloat16)
    d_z_weight, d_x_weight, d_bc_weight, d_dt_weight, d_out_weight = (
        lax.psum_scatter(d_z_weight, "fsdp", scatter_dimension=0, tiled=True),
        lax.psum_scatter(d_x_weight, "fsdp", scatter_dimension=0, tiled=True),
        lax.psum_scatter(d_bc_weight, "fsdp", scatter_dimension=0, tiled=True),
        lax.psum_scatter(d_dt_weight, "fsdp", scatter_dimension=0, tiled=True),
        lax.psum_scatter(d_out_weight, "fsdp", scatter_dimension=0, tiled=True),
    )
    (
        d_x_kernel,
        d_x_bias,
        d_bc_kernel,
        d_bc_bias,
        d_dt_bias,
        d_decay_log,
        d_skip_gain,
        d_out_gain,
    ) = lax.psum(
        (
            d_x_kernel,
            d_x_bias,
            d_bc_kernel,
            d_bc_bias,
            d_dt_bias,
            d_decay_log,
            d_skip_gain,
            d_out_gain,
        ),
        "fsdp",
    )
    d_norm_gain = lax.psum(d_norm_part, ("fsdp", "tp"))
    return (
        output,
        d_tokens,
        d_norm_gain,
        d_z_weight,
        d_x_weight,
        d_bc_weight,
        d_dt_weight,
        d_x_kernel,
        d_x_bias,
        d_bc_kernel,
        d_bc_bias,
        d_dt_bias,
        d_decay_log,
        d_skip_gain,
        d_out_gain,
        d_out_weight,
    )


def bits_of(count):
    return [1 << k for k in range(count.bit_length() - 1)]


def orders_of(fsdp_count, tp_count):
    own = bits_of(fsdp_count)
    other = [bit * fsdp_count for bit in bits_of(tp_count)]
    return (own[:2] + other + own[2:], own[:1] + other + own[1:])


def flipped(mask, fsdp_count, f_pos, t_pos):
    low, high = mask % fsdp_count, mask // fsdp_count
    for bit in bits_of(fsdp_count):
        if low & bit:
            f_pos = f_pos + bit - 2 * bit * ((lax.axis_index("fsdp") // bit) % 2)
    bit = 1
    while bit <= high:
        if high & bit:
            t_pos = t_pos + bit - 2 * bit * ((lax.axis_index("tp") // bit) % 2)
        bit *= 2
    return f_pos, t_pos


def greet(all_bits, place):
    barrier = pltpu.get_barrier_semaphore()
    for bit in all_bits:
        pl.semaphore_signal(
            barrier, inc=1, device_id=place(bit), device_id_type=pl.DeviceIdType.MESH
        )
    pl.semaphore_wait(barrier, len(all_bits))


def gather_kernel(
    fsdp_count, tp_count, shard, small, full, small_full, send_sem, recv_sem, near_sem,
    small_send, small_recv,
):
    f_own, t_own = lax.axis_index("fsdp"), lax.axis_index("tp")
    place = lambda mask: flipped(mask, fsdp_count, f_own, t_own)

    def slot(mask):
        f_pos, t_pos = place(mask)
        return t_pos * fsdp_count + f_pos

    total = fsdp_count * tp_count
    forward = orders_of(fsdp_count, tp_count)
    greet(forward[0], place)
    half = shard.shape[1] // 2
    pending = []

    def send(lane, mask, bit):
        cols = pl.ds(lane * half, half)
        source = shard.at[:, cols] if mask == 0 else full.at[slot(mask), :, cols]
        copy = pltpu.make_async_remote_copy(
            src_ref=source,
            dst_ref=full.at[slot(mask), :, cols],
            send_sem=send_sem.at[lane, mask + bit],
            recv_sem=recv_sem.at[lane, mask + bit],
            device_id=place(bit),
            device_id_type=pl.DeviceIdType.MESH,
        )
        copy.start()
        pending.append(copy)
        return copy

    arriving = {}
    orders = [list(reversed(order)) for order in forward]
    for lane in range(2):
        for bit in orders[lane]:
            arriving[lane, bit] = send(lane, 0, bit)
    near = pltpu.make_async_copy(shard, full.at[slot(0)], near_sem.at[0])
    near.start()
    near_small = pltpu.make_async_copy(small, small_full.at[t_own], near_sem.at[1])
    near_small.start()
    small_copies = []
    for t_mask in range(1, tp_count):
        copy = pltpu.make_async_remote_copy(
            src_ref=small,
            dst_ref=small_full.at[t_own],
            send_sem=small_send.at[t_mask],
            recv_sem=small_recv.at[t_mask],
            device_id=place(t_mask * fsdp_count),
            device_id_type=pl.DeviceIdType.MESH,
        )
        copy.start()
        small_copies.append(copy)
    held = [[0], [0]]
    for stage in range(len(forward[0])):
        for lane in range(2):
            bit = orders[lane][stage]
            later = orders[lane][stage + 1 :]
            for mask in list(held[lane]):
                arriving[lane, mask + bit].wait_recv()
                held[lane].append(mask + bit)
                for next_bit in later:
                    arriving[lane, mask + bit + next_bit] = send(lane, mask + bit, next_bit)
    for copy in small_copies:
        copy.wait()
    for copy in pending:
        copy.wait_send()
    near.wait()
    near_small.wait()


def gather_all(shard, small, fsdp_count, tp_count):
    total = fsdp_count * tp_count
    return pl.pallas_call(
        functools.partial(gather_kernel, fsdp_count, tp_count),
        out_shape=(
            jax.ShapeDtypeStruct((total,) + shard.shape, shard.dtype),
            jax.ShapeDtypeStruct((tp_count,) + small.shape, small.dtype),
        ),
        in_specs=[pl.BlockSpec(memory_space=pltpu.VMEM)] * 2,
        out_specs=(pl.BlockSpec(memory_space=pltpu.VMEM),) * 2,
        scratch_shapes=[
            pltpu.SemaphoreType.DMA((2, total)),
            pltpu.SemaphoreType.DMA((2, total)),
            pltpu.SemaphoreType.DMA((2,)),
            pltpu.SemaphoreType.DMA((tp_count,)),
            pltpu.SemaphoreType.DMA((tp_count,)),
        ],
        compiler_params=pltpu.CompilerParams(
            collective_id=0, has_side_effects=True, vmem_limit_bytes=40 << 20
        ),
        name="gather_weights",
    )(shard, small)


def reduce_kernel(
    fsdp_count, tp_count, lanes, first, second, small, first_out, second_out, small_out,
    first_got, second_got, first_sum, second_sum, small_sum, small_got,
    send_sem, recv_sem, small_send, small_recv,
):
    f_own, t_own = lax.axis_index("fsdp"), lax.axis_index("tp")
    place = lambda mask: flipped(mask, fsdp_count, f_own, t_own)

    def slot(mask):
        f_pos, t_pos = place(mask)
        return t_pos * fsdp_count + f_pos

    total = fsdp_count * tp_count
    both = orders_of(fsdp_count, tp_count)
    greet(both[0], place)
    parts = ((first, first_got, first_sum, first_out), (second, second_got, second_sum, second_out))
    stages = len(both[0])
    pending = []
    arriving = {}
    small_copies = []
    for stage in range(stages + 1):
        if stage < stages:
            bit = both[0][stage]
            source = small if stage == 0 else small_sum.at[stage - 1]
            small_copy = pltpu.make_async_remote_copy(
                src_ref=source,
                dst_ref=small_got.at[stage],
                send_sem=small_send.at[stage],
                recv_sem=small_recv.at[stage],
                device_id=place(bit),
                device_id_type=pl.DeviceIdType.MESH,
            )
            small_copy.start()
            pending.append(small_copy)
        for lane, (which, start, size, order_pos) in enumerate(lanes):
            given, got, held, out = parts[which]
            order = both[order_pos]
            cols = pl.ds(start, size)
            kept = [m for m in range(total) if not any(m & b for b in order[:stage])]
            if stage > 0:
                previous = order[stage - 1]
                now = order[stage] if stage < stages else 0
                kept = sorted(kept, key=lambda m: not (m & now))
            for mask in kept:
                if stage > 0:
                    arriving[lane, mask + previous].wait_recv()
                    before = given[slot(mask), :, cols] if stage == 1 else held[mask // 2, :, cols]
                    add = got[mask + previous, :, cols]
                    if stage == stages:
                        out[:, cols] = before.astype(jnp.float32) + add.astype(jnp.float32)
                    else:
                        held[mask // 2, :, cols] = before + add
                if stage < stages and mask & order[stage]:
                    source = (
                        given.at[slot(mask), :, cols]
                        if stage == 0
                        else held.at[mask // 2, :, cols]
                    )
                    copy = pltpu.make_async_remote_copy(
                        src_ref=source,
                        dst_ref=got.at[mask, :, cols],
                        send_sem=send_sem.at[lane, mask],
                        recv_sem=recv_sem.at[lane, mask],
                        device_id=place(order[stage]),
                        device_id_type=pl.DeviceIdType.MESH,
                    )
                    copy.start()
                    pending.append(copy)
                    arriving[lane, mask] = copy
        if stage < stages:
            small_copy.wait_recv()
            before = small[...] if stage == 0 else small_sum[stage - 1]
            if stage == stages - 1:
                small_out[...] = before + small_got[stage]
            else:
                small_sum[stage] = before + small_got[stage]
    for copy in pending:
        copy.wait_send()


def reduce_all(first, second, small, fsdp_count, tp_count):
    total, rows, wide = first.shape
    narrow = second.shape[2]
    cut = (wide * 3 // 5) // 128 * 128
    lanes = ((1, 0, narrow, 0), (0, 0, cut, 1), (0, cut, wide - cut, 0))
    stages = total.bit_length() - 1
    low = jnp.bfloat16
    return pl.pallas_call(
        functools.partial(reduce_kernel, fsdp_count, tp_count, lanes),
        out_shape=(
            jax.ShapeDtypeStruct((rows, wide), jnp.float32),
            jax.ShapeDtypeStruct((rows, narrow), jnp.float32),
            jax.ShapeDtypeStruct(small.shape, jnp.float32),
        ),
        in_specs=[pl.BlockSpec(memory_space=pltpu.VMEM)] * 3,
        out_specs=(pl.BlockSpec(memory_space=pltpu.VMEM),) * 3,
        scratch_shapes=[
            pltpu.VMEM((total, rows, wide), low),
            pltpu.VMEM((total, rows, narrow), low),
            pltpu.VMEM((total // 2, rows, wide), low),
            pltpu.VMEM((total // 2, rows, narrow), low),
            pltpu.VMEM((stages,) + small.shape, jnp.float32),
            pltpu.VMEM((stages,) + small.shape, jnp.float32),
            pltpu.SemaphoreType.DMA((len(lanes), total)),
            pltpu.SemaphoreType.DMA((len(lanes), total)),
            pltpu.SemaphoreType.DMA((stages,)),
            pltpu.SemaphoreType.DMA((stages,)),
        ],
        compiler_params=pltpu.CompilerParams(
            collective_id=1, has_side_effects=True, vmem_limit_bytes=48 << 20
        ),
        name="reduce_gradients",
    )(first, second, small)


def pad_cols(value, width):
    return jnp.pad(value, ((0, 0), (0, width - value.shape[1])))


def by_sequence(
    fsdp_count,
    tp_count,
    tokens,
    norm_gain,
    z_weight,
    x_weight,
    bc_weight,
    dt_weight,
    x_kernel,
    x_bias,
    bc_kernel,
    bc_bias,
    dt_bias,
    decay_log,
    skip_gain,
    out_gain,
    out_weight,
    cotangent,
):
    rows, width = z_weight.shape
    heads = dt_weight.shape[1]
    depth = tokens.shape[1]
    count = tokens.shape[0]
    bc_share = 2 * NSTATE // tp_count
    bc_own = lax.dynamic_slice_in_dim(bc_weight, lax.axis_index("tp") * bc_share, bc_share, 1)
    shard = jnp.concatenate(
        [z_weight, x_weight, pad_cols(dt_weight, DT_PAD), bc_own, out_weight], 1
    )
    small = jnp.concatenate(
        [
            x_kernel,
            x_bias[None],
            out_gain[None],
            pad_cols(jnp.concatenate([dt_bias, decay_log, skip_gain])[None], width),
            jnp.zeros((1, width), jnp.float32),
        ],
        0,
    )
    full, small_full = gather_all(shard, small, fsdp_count, tp_count)
    full = full.reshape(tp_count, depth, shard.shape[1])
    out_start = 2 * width + DT_PAD + bc_share
    proj_w, out_w = full[:, :, :out_start], full[:, :, out_start:]
    join = lambda value: jnp.moveaxis(value, 0, -2).reshape(value.shape[1:-1] + (-1,))
    out_gain_all = small_full[:, CONV + 1]
    tiny = small_full[:, CONV + 2, : 3 * heads].reshape(tp_count, 3, heads)
    dt_bias_all, decay_all, skip_all = (tiny[:, k].reshape(-1) for k in range(3))

    residual = tokens.astype(jnp.float32)
    normed, norm_pull = jax.vjp(prenorm, residual, norm_gain)
    normed_low = normed.astype(jnp.bfloat16)
    raw = jnp.einsum(
        "rk,tkc->trc", normed_low, proj_w, preferred_element_type=jnp.float32
    ).astype(jnp.bfloat16)
    dtraw_low = join(raw[:, :, 2 * width : 2 * width + heads])
    bcraw_low = join(raw[:, :, 2 * width + DT_PAD :])
    bc_conv, conv_pull = jax.vjp(
        causal_conv, bcraw_low.astype(jnp.float32)[None], bc_kernel, bc_bias
    )
    gated, scan_pull = mixer_by_pairs(
        raw, small_full, bc_conv[0].astype(jnp.bfloat16), dtraw_low, dt_bias_all, decay_all,
        skip_all,
    )
    scale = lax.rsqrt(jnp.sum(gated * gated, (0, 2)) / INNER + epsilon)[:, None]
    gain = out_gain_all[:, None]
    mixed_low = (gated * scale * gain).astype(jnp.bfloat16)
    split = lambda value: jnp.moveaxis(value.reshape(value.shape[0], tp_count, -1), 1, 0)
    branch = jnp.einsum("trc,tkc->rk", mixed_low, out_w, preferred_element_type=jnp.float32)
    output = (residual + branch).astype(jnp.bfloat16)
    d_out_weight = jnp.einsum(
        "rk,trc->tkc", cotangent, mixed_low, preferred_element_type=jnp.float32
    ).astype(jnp.bfloat16)
    d_mixed = jnp.einsum("rk,tkc->trc", cotangent, out_w, preferred_element_type=jnp.float32)
    d_out_gain = jnp.sum(d_mixed * gated * scale, 1)
    scaled_grad = d_mixed * gain
    cross_sum = jnp.sum(scaled_grad * gated, (0, 2))
    d_gated = scale * scaled_grad - gated * scale**3 * (cross_sum / INNER)[:, None]
    (
        xraw_grad, d_bc_round, d_dt_raw, gate_grad, d_dt_bias, d_decay_log, d_skip_gain, d_taps,
    ) = scan_pull(d_gated)
    d_bc_raw, d_bc_kernel, d_bc_bias = conv_pull(d_bc_round[None])
    d_bc_raw = d_bc_raw[0]
    d_x_kernel = jnp.moveaxis(d_taps[:, :CONV], 1, 0)
    d_x_bias = d_taps[:, CONV]
    low = jnp.bfloat16
    bc_grad = d_bc_raw.astype(low)
    dt_grad = split(d_dt_raw.astype(low))
    dt_grad = jnp.pad(dt_grad, ((0, 0), (0, 0), (0, DT_PAD - heads)))
    lead = jnp.concatenate([gate_grad, xraw_grad, dt_grad], 2)
    proj_grad = jnp.concatenate([lead, split(bc_grad)], 2)
    d_normed = jnp.einsum("trc,tkc->rk", proj_grad, proj_w, preferred_element_type=jnp.float32)
    bc_all = jnp.broadcast_to(bc_grad[None], (tp_count,) + bc_grad.shape)
    d_proj = jnp.einsum(
        "rk,trc->tkc",
        normed_low,
        jnp.concatenate([lead, bc_all], 2),
        preferred_element_type=jnp.float32,
    ).astype(low)
    d_residual, d_norm_gain = norm_pull(d_normed)
    d_tokens = (cotangent.astype(jnp.float32) + d_residual).astype(jnp.bfloat16)
    tiny_grad = jnp.stack([d_dt_bias, d_decay_log, d_skip_gain]).reshape(3, tp_count, heads)
    tiny_grad = jnp.moveaxis(tiny_grad, 1, 0).reshape(tp_count, 3 * heads)
    flat = jnp.concatenate(
        [
            d_norm_gain,
            d_bc_kernel.reshape(-1),
            d_bc_bias,
            d_out_gain.reshape(-1),
            d_x_bias.reshape(-1),
            d_x_kernel.reshape(-1),
            tiny_grad.reshape(-1),
        ]
    )
    lines = -(-flat.size // width)
    lines = -(-lines // 8) * 8
    small_grad = jnp.pad(flat, (0, lines * width - flat.size)).reshape(lines, width)
    wide, narrow, sums = reduce_all(
        d_proj.reshape(fsdp_count * tp_count, rows, -1),
        d_out_weight.reshape(fsdp_count * tp_count, rows, -1),
        small_grad,
        fsdp_count,
        tp_count,
    )
    sums = sums.reshape(-1)
    t_own = lax.axis_index("tp")
    position = 0

    def take(*shape):
        nonlocal position
        size = 1
        for extent in shape:
            size *= extent
        piece = sums[position : position + size].reshape(shape)
        position += size
        return piece

    own = lambda value: lax.dynamic_index_in_dim(value, t_own, value.ndim - 2, keepdims=False)
    d_norm_gain = take(depth)
    d_bc_kernel = take(CONV, 2 * NSTATE)
    d_bc_bias = take(2 * NSTATE)
    d_out_gain = own(take(tp_count, width))
    d_x_bias = own(take(tp_count, width))
    d_x_kernel = own(take(CONV, tp_count, width))
    d_tiny = own(take(tp_count, 3 * heads)).reshape(3, heads)
    return (
        output,
        d_tokens,
        d_norm_gain,
        wide[:, :width],
        wide[:, width : 2 * width],
        wide[:, 2 * width + DT_PAD :],
        wide[:, 2 * width : 2 * width + heads],
        d_x_kernel,
        d_x_bias,
        d_bc_kernel,
        d_bc_bias,
        d_tiny[0],
        d_tiny[1],
        d_tiny[2],
        d_out_gain,
        narrow,
    )


def moved(value, shift):
    if shift == 0:
        return value
    count = value.shape[0]
    row = lax.broadcasted_iota(jnp.int32, value.shape, 0)
    inside = row >= shift if shift > 0 else row < count + shift
    return jnp.where(inside, pltpu.roll(value, shift % count, 0), 0.0)


def pair_conv(raw_ref, taps_ref):
    raw = raw_ref[0].astype(jnp.float32)
    shifted = [moved(raw, CONV - 1 - k) for k in range(CONV)]
    before = taps_ref[0, CONV : CONV + 1]
    for k in range(CONV):
        before = before + taps_ref[0, k : k + 1] * shifted[k]
    sigmoid = 1.0 / (1.0 + jnp.exp(-before))
    return (before * sigmoid).astype(jnp.bfloat16).astype(jnp.float32), before, sigmoid, shifted


def pair_parts(x_all, cum_ref, cum_row_ref, dt_ref, b_ref, c_ref, scores):
    size = SCAN_BLOCK
    lane = lax.broadcasted_iota(jnp.int32, (size, 2 * HEADDIM), 1)
    left = lane < HEADDIM
    causal = lax.broadcasted_iota(jnp.int32, (size, size), 0) >= lax.broadcasted_iota(
        jnp.int32, (size, size), 1
    )
    spread = lambda pair: jnp.where(left, pair[:, 0:1], pair[:, 1:2])
    parts = []
    for block in range(2):
        rows = slice(block * size, (block + 1) * size)
        cum, dt = cum_ref[0, rows], dt_ref[0, rows]
        x = x_all[rows]
        scaled = x * spread(dt)
        masks, mixes = [], []
        for head in range(2):
            gaps = cum[:, head : head + 1] - cum_row_ref[0, head : head + 1, rows]
            mask = jnp.exp(jnp.where(causal, gaps, -1e30))
            masks.append(mask)
            mixes.append(scores[block] * mask)
        parts.append((rows, cum, dt, x, scaled, masks, mixes))
    return left, spread, parts


def dot_of(left, right, left_dim, right_dim):
    low = jnp.bfloat16
    return lax.dot_general(
        left.astype(low),
        right.astype(low),
        (((left_dim,), (right_dim,)), ((), ())),
        preferred_element_type=jnp.float32,
    )


def head_outputs(left, spread, parts, b_ref, c_ref):
    found = []
    for rows, cum, dt, x, scaled, masks, mixes in parts:
        found.append(
            dot_of(mixes[0], jnp.where(left, scaled, 0.0), 1, 0)
            + dot_of(mixes[1], jnp.where(left, 0.0, scaled), 1, 0)
        )
    rows, cum, dt, x, scaled, masks, mixes = parts[0]
    to_end = jnp.exp(spread(cum[SCAN_BLOCK - 1 : SCAN_BLOCK] - cum))
    ended = to_end * scaled
    state = dot_of(b_ref[rows], ended, 0, 0)
    later = parts[1][0]
    growth = jnp.exp(spread(parts[1][1]))
    across = growth * dot_of(c_ref[later], state, 1, 0)
    found[1] = found[1] + across
    return found, state, to_end, ended, growth, across


def fill_scores(scores, b_ref, c_ref):
    for block in range(2):
        rows = slice(block * SCAN_BLOCK, (block + 1) * SCAN_BLOCK)
        scores[block] = dot_of(c_ref[rows], b_ref[rows], 1, 1)


def scan_forward(
    raw_ref, gate_ref, b_ref, c_ref, cum_ref, cum_row_ref, dt_ref, skip_ref, taps_ref, gated_ref,
    scores,
):
    @pl.when(pl.program_id(0) == 0)
    def _():
        fill_scores(scores, b_ref, c_ref)

    x_all, before, conv_sigmoid, shifted = pair_conv(raw_ref, taps_ref)
    left, spread, parts = pair_parts(x_all, cum_ref, cum_row_ref, dt_ref, b_ref, c_ref, scores)
    found = head_outputs(left, spread, parts, b_ref, c_ref)[0]
    for block in range(2):
        rows, x = parts[block][0], parts[block][3]
        gate = gate_ref[0, rows].astype(jnp.float32)
        gated_ref[0, rows] = (found[block] + skip_ref[0] * x) * (gate / (1.0 + jnp.exp(-gate)))


def scan_backward(
    raw_ref, gate_ref, b_ref, c_ref, cum_ref, cum_row_ref, dt_ref, skip_ref, taps_ref, grad_ref,
    d_raw_ref, d_gate_ref, d_b_ref, d_c_ref, d_cols_ref, d_row_ref, d_taps_ref,
    scores, d_scores,
):
    step = pl.program_id(0)

    @pl.when(step == 0)
    def _():
        fill_scores(scores, b_ref, c_ref)
        d_scores[...] = jnp.zeros_like(d_scores)
        d_b_ref[...] = jnp.zeros_like(d_b_ref)
        d_c_ref[...] = jnp.zeros_like(d_c_ref)

    x_all, before, conv_sigmoid, shifted = pair_conv(raw_ref, taps_ref)
    left, spread, parts = pair_parts(x_all, cum_ref, cum_row_ref, dt_ref, b_ref, c_ref, scores)
    found, state, to_end, ended, growth, across = head_outputs(left, spread, parts, b_ref, c_ref)
    skip = skip_ref[0]
    grads, d_scaled, d_cum = [], [], []
    d_skip = jnp.zeros((1, 2 * HEADDIM), jnp.float32)

    def per_head(value):
        return (
            jnp.sum(jnp.where(left, value, 0.0), 1, keepdims=True),
            jnp.sum(jnp.where(left, 0.0, value), 1, keepdims=True),
        )

    for block in range(2):
        rows, cum, dt, x, scaled, masks, mixes = parts[block]
        gate = gate_ref[0, rows].astype(jnp.float32)
        sigmoid = 1.0 / (1.0 + jnp.exp(-gate))
        outer = grad_ref[0, rows]
        inner = found[block] + skip * x
        d_gate = outer * inner * sigmoid * (1.0 + gate * (1.0 - sigmoid))
        d_gate_ref[0, rows] = d_gate.astype(d_gate_ref.dtype)
        grad = outer * gate * sigmoid
        d_skip = d_skip + jnp.sum(grad * x, 0, keepdims=True)
        halves = (jnp.where(left, grad, 0.0), jnp.where(left, 0.0, grad))
        back = jnp.zeros_like(grad)
        sums = []
        total = jnp.zeros((SCAN_BLOCK, SCAN_BLOCK), jnp.float32)
        for head in range(2):
            d_mix = dot_of(halves[head], scaled, 1, 1)
            total = total + d_mix * masks[head]
            both = d_mix * mixes[head]
            sums.append(jnp.sum(both, 1, keepdims=True))
            d_row_ref[0, head : head + 1, rows] = jnp.sum(both, 0, keepdims=True)
            back = back + dot_of(mixes[head], halves[head], 0, 0)
        d_scores[block] += total
        grads.append(grad)
        d_scaled.append(back)
        d_cum.append(sums)
    later, early = parts[1][0], parts[0][0]
    d_across = grads[1] * growth
    d_c_ref[later] += dot_of(d_across, state, 1, 1)
    d_state = dot_of(c_ref[later], d_across, 0, 0)
    extra = per_head(grads[1] * across)
    d_cum[1] = [d_cum[1][head] + extra[head] for head in range(2)]
    d_ended = dot_of(b_ref[early], d_state, 1, 0)
    d_b_ref[early] += dot_of(ended, d_state, 1, 1)
    d_scaled[0] = d_scaled[0] + d_ended * to_end
    decayed = per_head(d_ended * ended)
    last = lax.broadcasted_iota(jnp.int32, (SCAN_BLOCK, 1), 0) == SCAN_BLOCK - 1
    d_cum[0] = [
        d_cum[0][head]
        - decayed[head]
        + jnp.where(last, jnp.sum(decayed[head], 0, keepdims=True), 0.0)
        for head in range(2)
    ]
    d_x = []
    spot = lax.broadcasted_iota(jnp.int32, (SCAN_BLOCK, 4), 1)
    for block in range(2):
        rows, cum, dt, x, scaled, masks, mixes = parts[block]
        d_x.append(d_scaled[block] * spread(dt) + skip * grads[block])
        d_dt = per_head(d_scaled[block] * x)
        d_cols_ref[0, rows] = jnp.where(
            spot < 2,
            jnp.where(spot == 0, d_cum[block][0], d_cum[block][1]),
            jnp.where(spot == 2, d_dt[0], d_dt[1]),
        )
    d_before = (
        jnp.concatenate(d_x, 0) * conv_sigmoid * (1.0 + before * (1.0 - conv_sigmoid))
    )
    d_raw = jnp.zeros_like(d_before)
    for k in range(CONV):
        d_raw = d_raw + taps_ref[0, k : k + 1] * moved(d_before, k + 1 - CONV)
        d_taps_ref[0, k : k + 1] = jnp.sum(d_before * shifted[k], 0, keepdims=True)
    d_raw_ref[0] = d_raw.astype(d_raw_ref.dtype)
    d_taps_ref[0, CONV : CONV + 1] = jnp.sum(d_before, 0, keepdims=True)
    d_taps_ref[0, CONV + 1 : CONV + 2] = d_skip
    d_taps_ref[0, CONV + 2 :] = jnp.zeros((8 - CONV - 2, 2 * HEADDIM), jnp.float32)

    @pl.when(step == pl.num_programs(0) - 1)
    def _():
        for block in range(2):
            rows = slice(block * SCAN_BLOCK, (block + 1) * SCAN_BLOCK)
            d_c_ref[rows] += dot_of(d_scores[block], b_ref[rows], 1, 0)
            d_b_ref[rows] += dot_of(d_scores[block], c_ref[rows], 0, 0)


def steps_of(dt_raw, dt_bias, decay_log):
    delta = jax.nn.softplus(dt_raw + dt_bias)
    places = jnp.arange(SCAN_BLOCK)
    causal = (places[:, None] >= places[None, :]).astype(jnp.float32)
    steps = (delta * -jnp.exp(decay_log)).reshape(-1, SCAN_BLOCK, delta.shape[1])
    cum = jnp.einsum("qr,krh->kqh", causal, steps, precision=highest)
    return delta, cum.reshape(delta.shape)


def mixer_by_pairs(raw, taps, bc_conv, dt_raw, dt_bias, decay_log, skip_gain):
    tp_count, count = raw.shape[:2]
    width = taps.shape[2]
    per = width // (2 * HEADDIM)
    pairs = tp_count * per
    (delta, cum), steps_pull = jax.vjp(steps_of, dt_raw.astype(jnp.float32), dt_bias, decay_log)
    paired = lambda value: jnp.moveaxis(value.reshape(count, pairs, 2), 1, 0)
    skip = jnp.repeat(skip_gain, HEADDIM).reshape(pairs, 1, 2 * HEADDIM)
    cum_col = paired(cum)
    given = (
        raw, raw, bc_conv, bc_conv, cum_col, jnp.swapaxes(cum_col, 1, 2), paired(delta), skip,
        taps,
    )
    tile = lambda rows, start: pl.BlockSpec(
        (1, rows, 2 * HEADDIM), lambda j: (j // per, 0, start + j % per)
    )
    own = tile(count, 0)
    whole = lambda place: pl.BlockSpec((count, NSTATE), lambda j: (0, place))
    column = pl.BlockSpec((1, count, 2), lambda j: (j, 0, 0))
    line = pl.BlockSpec((1, 2, count), lambda j: (j, 0, 0))
    single = pl.BlockSpec((1, 1, 2 * HEADDIM), lambda j: (j, 0, 0))
    specs = [
        tile(count, per), own, whole(0), whole(1), column, line, column, single, tile(8, 0)
    ]
    square = pltpu.VMEM((2, SCAN_BLOCK, SCAN_BLOCK), jnp.float32)
    params = pltpu.CompilerParams(vmem_limit_bytes=32 << 20)
    full = jax.ShapeDtypeStruct
    gated = pl.pallas_call(
        scan_forward,
        grid=(pairs,),
        in_specs=specs,
        out_specs=own,
        out_shape=full((tp_count, count, width), jnp.float32),
        scratch_shapes=[square],
        compiler_params=params,
        name="scan_forward",
    )(*given)

    def pull(d_gated):
        d_raw, d_gate, d_b, d_c, d_cols, d_row, d_taps = pl.pallas_call(
            scan_backward,
            grid=(pairs,),
            in_specs=specs + [own],
            out_specs=(
                own, own, whole(0), whole(0), pl.BlockSpec((1, count, 4), lambda j: (j, 0, 0)),
                line, tile(8, 0),
            ),
            out_shape=(
                full((tp_count, count, width), jnp.bfloat16),
                full((tp_count, count, width), jnp.bfloat16),
                full((count, NSTATE), jnp.float32),
                full((count, NSTATE), jnp.float32),
                full((pairs, count, 4), jnp.float32),
                full((pairs, 2, count), jnp.float32),
                full((tp_count, 8, width), jnp.float32),
            ),
            scratch_shapes=[square, square],
            compiler_params=params,
            name="scan_backward",
        )(*given, d_gated)
        merged = lambda value: jnp.moveaxis(value, 0, 1).reshape(count, 2 * pairs)
        d_cum = merged(d_cols[:, :, :2] - jnp.swapaxes(d_row, 1, 2))
        d_dt_raw, d_dt_bias, d_decay_log = steps_pull((merged(d_cols[:, :, 2:]), d_cum))
        d_skip_gain = jnp.sum(d_taps[:, CONV + 1].reshape(2 * pairs, HEADDIM), 1)
        return (
            d_raw, jnp.concatenate([d_b, d_c], 1), d_dt_raw, d_gate, d_dt_bias, d_decay_log,
            d_skip_gain, d_taps,
        )

    return gated, pull


def solution(mesh):
    placed = (
        P(("fsdp", "tp"), None),
        P(),
        P("fsdp", "tp"),
        P("fsdp", "tp"),
        P("fsdp", None),
        P("fsdp", "tp"),
        P(None, "tp"),
        P("tp"),
        P(),
        P(),
        P("tp"),
        P("tp"),
        P("tp"),
        P("tp"),
        P("fsdp", "tp"),
        P(("fsdp", "tp"), None),
    )
    fsdp_count, tp_count = mesh.shape["fsdp"], mesh.shape["tp"]
    total = fsdp_count * tp_count

    def program(*arrays):
        rows, width = arrays[2].shape
        whole = arrays[0].shape[0] == LEN == 2 * SCAN_BLOCK and 2 * NSTATE % (128 * tp_count) == 0
        tiled = rows % 16 == 0 and width % 128 == 0 and arrays[0].shape[1] == width
        if whole and tiled and total & (total - 1) == 0 and fsdp_count >= 4:
            return by_sequence(fsdp_count, tp_count, *arrays)
        return local(*arrays)

    return jax.shard_map(
        program,
        mesh=mesh,
        in_specs=placed,
        out_specs=(
            P(("fsdp", "tp"), None),
            P(("fsdp", "tp"), None),
            P(),
            P("fsdp", "tp"),
            P("fsdp", "tp"),
            P("fsdp", None),
            P("fsdp", "tp"),
            P(None, "tp"),
            P("tp"),
            P(),
            P(),
            P("tp"),
            P("tp"),
            P("tp"),
            P("tp"),
            P("fsdp", "tp"),
        ),
        check_vma=False,
    )
```
